512 devices in a mesh: prefix: 64 (over z, x), tensor: 8 (over y, core).
Axes of the slice: x: 4, y: 4, z: 16, core: 2. Of those that a mesh axis runs over, the one named last changes fastest.
Arguments:
- queries: bfloat16 [4096, 8192], P(('prefix', 'tensor')), may hold values from -24 to 24
- suffix_kv: bfloat16 [4096, 2, 8, 64, 128], P('prefix', None, 'tensor'), may hold values from -15 to 15
- suffix_lengths: int32 [4096], P('prefix'), may hold values from 1 to 64
- prefix_kv: bfloat16 [64, 2, 8, 4096, 128], P('prefix', None, 'tensor'), may hold values from -16 to 16
- tree_ids: int32 [4096], P('prefix'), may hold values from 0 to 63, as said below
- owner_map: int32 [64], replicated, may hold values from 0 to 63, as said below
Outputs:
- attended: bfloat16 [4096, 8192], P(('prefix', 'tensor'))
The draws below stay inside these ranges and needn't reach their ends.
Inputs may be any that keep to these rules, and one draw needn't show every extreme that they name: `tree_ids`: in each aligned block of 64 rows (the rows of one index of prefix) no prompt is named by more than 2 rows, and some prompt is named by exactly 2 rows in every block. `owner_map`: A permutation: every row of prefix_kv holds the prefix of exactly one prompt.
All inputs are finite; a program needn't handle non-finite values.
Results may differ from the reference program's by a relative error of at most 0.0017.
Values may be sent and summed in bfloat16 or wider, within the bound.
No kernel may reach another device: no remote copies, remote signals or barrier semaphores. Data moves between devices by JAX's collectives and lax.ppermute only.
A program may use at most 64 MiB of HBM per device.

```python
import math
import jax
import jax.numpy as jnp
from jax import lax

H = 64
KVH = 8
HD = 128
PLEN = 4096
SUF = 64
ROWS_DEV = 64
PREFIXES = 64
ROWS = 4096
MOST = 2


def tree_layout(key):
    base_key = jax.random.fold_in(key, 101)
    hot_key, pick_key = jax.random.split(base_key)
    candidates = PREFIXES * MOST
    cand_prompt = jnp.arange(candidates, dtype=jnp.int32) // MOST
    hottest = jax.random.randint(hot_key, (), 0, PREFIXES, dtype=jnp.int32)
    popular = (cand_prompt * 5 + hottest) % 4 == 0

    def one_block(block_key):
        order_key, shuffle_key = jax.random.split(block_key)
        ranking = jax.random.permutation(order_key, candidates).astype(jnp.int32)
        ranking = ranking - jnp.where(popular, candidates, 0) - jnp.where(cand_prompt == hottest, 2 * candidates, 0)
        chosen = jnp.argsort(ranking, stable=True)[:ROWS_DEV]
        return jax.random.permutation(shuffle_key, cand_prompt[chosen])
    layout = jax.vmap(one_block)(jax.random.split(pick_key, PREFIXES))
    return layout.reshape(-1).astype(jnp.int32)


def owner_layout(key):
    return jax.random.permutation(jax.random.fold_in(key, 202), PREFIXES).astype(jnp.int32)


def draw_tree_ids(key, part):
    return tree_layout(key)


def draw_owner_map(key, part):
    return owner_layout(key)


def draw_queries(key, part):
    base_key = jax.random.fold_in(key, 505)
    drawn = jax.random.normal(base_key, (ROWS, H * HD), jnp.float32)
    return jnp.clip(drawn, -6.0, 6.0).astype(jnp.bfloat16)


def draw_prefix_kv(key, part):
    base_key = jax.random.fold_in(key, 606)
    shape = (PREFIXES, 2, KVH, PLEN, HD)
    drawn = 0.6 * jax.random.normal(base_key, shape, jnp.float32)
    return jnp.clip(drawn, -3.6, 3.6).astype(jnp.bfloat16)


def with_ends(result, stream_key, low, top_value):
    index_at = [jax.random.randint(jax.random.fold_in(stream_key, axis), (), 0, length) for axis, length in enumerate(result.shape)]
    longest = result.shape.index(max(result.shape))
    beside = index_at[:longest] + [(index_at[longest] + 1) % result.shape[longest]] + index_at[longest + 1:]
    return result.at[tuple(index_at)].set(low).at[tuple(beside)].set(top_value)


def shard_levels(own_key, dims, shards, least, high):
    level = 1.0
    for dim, parts in shards:
        steps = jax.random.uniform(jax.random.fold_in(jax.random.fold_in(own_key, 6), dim), (parts,), jnp.float32, least / len(shards), high / len(shards))
        level = level * jnp.repeat(jnp.exp(steps), dims[dim] // parts).reshape((-1,) + (1,) * (len(dims) - 1 - dim))
    return level


def noise(stream_key, dims, deviation, bound, cuts=(), kind=jnp.bfloat16):
    values = jax.random.normal(stream_key, dims, jnp.float32) * deviation
    if len(cuts) > 0:
        values = shard_levels(stream_key, dims, cuts, -0.22, 0.18) * values
    return jnp.clip(values, min=-bound, max=bound).astype(kind)


def setup_inputs(seed: int = 0) -> dict:
    key_list = jax.random.split(jax.random.key(seed), 7)
    return {
        "queries": draw_queries(jax.random.fold_in(key_list[6], 71), 0),
        "suffix_kv": noise(key_list[1], (ROWS, 2, KVH, SUF, HD), 2.5, 15.0, ((0, 64), (2, 8))),
        "suffix_lengths": with_ends(jax.random.randint(key_list[2], (ROWS,), 1, SUF + 1), jax.random.fold_in(key_list[2], 1), 1, SUF).astype(jnp.int32),
        "prefix_kv": draw_prefix_kv(jax.random.fold_in(key_list[6], 71), 0),
        "tree_ids": draw_tree_ids(jax.random.fold_in(key_list[6], 71), 0),
        "owner_map": draw_owner_map(jax.random.fold_in(key_list[6], 71), 0),
    }


def rounded_f32(weights):
    return lax.optimization_barrier(weights.astype(jnp.bfloat16)).astype(jnp.float32)

def suffix_block(packed):
    query_rows, cache_rows, length_rows = packed
    score_scale = 1.0 / math.sqrt(HD)
    cache_f32 = cache_rows.astype(jnp.float32)
    suffix_scores = jnp.einsum('rgid,rgnd->rgin', query_rows, cache_f32[:, 0]) * score_scale
    position = jnp.arange(SUF, dtype=jnp.int32)
    is_live = (position[None, :] < length_rows[:, None])[:, None, None, :]
    suffix_top = lax.optimization_barrier(jnp.max(jnp.where(is_live, suffix_scores, -jnp.inf), axis=-1))
    suffix_weights = jnp.where(is_live, jnp.exp(suffix_scores - suffix_top[..., None]), 0.0)
    suffix_total = lax.optimization_barrier(jnp.sum(suffix_weights, axis=-1))
    suffix_sum = jnp.einsum('rgin,rgnd->rgid', rounded_f32(suffix_weights), cache_f32[:, 1])
    return (suffix_top, suffix_total, suffix_sum)

def reference(queries, suffix_kv, suffix_lengths, prefix_kv, tree_ids, owner_map):
    group_size = H // KVH
    score_scale = 1.0 / math.sqrt(HD)
    query_f32 = queries.astype(jnp.float32).reshape(ROWS, KVH, group_size, HD)
    stored = jnp.take(owner_map, tree_ids).astype(jnp.int32)
    capacity = PREFIXES * MOST

    def one_prefix(running, stored_index):
        part_all, top_all, total_all = running
        picked = jnp.argsort((stored != stored_index).astype(jnp.int32), stable=True)[:capacity].astype(jnp.int32)
        is_valid = stored[picked] == stored_index
        prefix_f32 = lax.dynamic_index_in_dim(prefix_kv, stored_index, 0, keepdims=False).astype(jnp.float32)
        chosen = query_f32[picked]
        scores = jnp.einsum('rgid,gnd->rgin', chosen, prefix_f32[0]) * score_scale
        row_top = lax.optimization_barrier(jnp.max(scores, axis=-1))
        weights = jnp.exp(scores - row_top[..., None])
        mass_sum = lax.optimization_barrier(jnp.sum(weights, axis=-1))
        prefix_part = jnp.einsum('rgin,gnd->rgid', rounded_f32(weights), prefix_f32[1]) / mass_sum[..., None]
        keep_rows = is_valid[:, None, None]
        part_all = part_all.at[picked].add(jnp.where(keep_rows[..., None], prefix_part, 0.0))
        top_all = top_all.at[picked].add(jnp.where(keep_rows, row_top, 0.0))
        total_all = total_all.at[picked].add(jnp.where(keep_rows, mass_sum, 0.0))
        return ((part_all, top_all, total_all), None)
    starting = (jnp.zeros((ROWS, KVH, group_size, HD), jnp.float32), jnp.zeros((ROWS, KVH, group_size), jnp.float32), jnp.zeros((ROWS, KVH, group_size), jnp.float32))
    (prefix_part, prefix_top, prefix_total), unused = lax.scan(one_prefix, starting, jnp.arange(PREFIXES, dtype=jnp.int32))
    blocks = ROWS // ROWS_DEV
    suffix_top, suffix_total, suffix_sum = lax.map(suffix_block, (query_f32.reshape(blocks, ROWS_DEV, KVH, group_size, HD), suffix_kv.reshape(blocks, ROWS_DEV, 2, KVH, SUF, HD), suffix_lengths.reshape(blocks, ROWS_DEV)))
    suffix_top = suffix_top.reshape(ROWS, KVH, group_size)
    suffix_total = suffix_total.reshape(ROWS, KVH, group_size)
    suffix_sum = suffix_sum.reshape(ROWS, KVH, group_size, HD)
    joint_top = jnp.maximum(prefix_top, suffix_top)
    prefix_mass = prefix_total * jnp.exp(prefix_top - joint_top)
    suffix_mass = jnp.exp(suffix_top - joint_top)
    attended = (prefix_mass[..., None] * prefix_part + suffix_mass[..., None] * suffix_sum) / (prefix_mass + suffix_mass * suffix_total)[..., None]
    return attended.reshape(ROWS, H * HD).astype(jnp.bfloat16)
```

```python
import math

import jax
import jax.numpy as jnp
from jax import lax
from jax.experimental import pallas as pl
from jax.experimental.pallas import tpu as pltpu
from jax.sharding import PartitionSpec as P

H = 64
KVH = 8
HD = 128
GROUP = H // KVH
SLOTS = 2
CODE_TOP = 32767.0
SCORE_SCALE = math.log2(math.e) / math.sqrt(HD)

BLOCK = 128
CHUNK = 512

NT = (((1,), (1,)), ((), ()))


def dispatch_kernel(slot_ref, q_ref, out_ref, home_ref, tile_ref):
    tensor, rows, width = q_ref.shape
    for t in range(tensor):
        for h in range(GROUP):
            tile_ref[pl.ds((t * GROUP + h) * rows, rows), :] = q_ref[
                t, :, h * HD : (h + 1) * HD
            ].astype(jnp.float32)
    for r in range(0, tensor * rows, 2):
        pair = []
        for k in range(2):
            t, i = divmod(r + k, rows)
            tile = tile_ref[pl.ds(t * GROUP * rows + i, GROUP, stride=rows), :]
            pair.append(tile)
            out_ref[slot_ref[r + k]] = tile.astype(jnp.bfloat16)
        home_ref[r // 2] = jnp.concatenate(pair, axis=0).astype(jnp.bfloat16)


def dispatch(slot, q_rows):
    tensor, rows, width = q_rows.shape
    count = tensor * rows
    owners = count
    return pl.pallas_call(
        dispatch_kernel,
        out_shape=(
            jax.ShapeDtypeStruct((owners * SLOTS, GROUP, HD), jnp.bfloat16),
            jax.ShapeDtypeStruct((count // 2, 2 * GROUP, HD), jnp.bfloat16),
        ),
        in_specs=[
            pl.BlockSpec(memory_space=pltpu.SMEM),
            pl.BlockSpec(memory_space=pltpu.VMEM),
        ],
        out_specs=(
            pl.BlockSpec(memory_space=pltpu.VMEM),
            pl.BlockSpec(memory_space=pltpu.VMEM),
        ),
        scratch_shapes=[pltpu.VMEM((count * GROUP, HD), jnp.float32)],
        compiler_params=pltpu.CompilerParams(vmem_limit_bytes=8 << 20),
        name="dispatch",
    )(slot, q_rows)


def suffix_kernel(length_ref, q_ref, kv_ref, sum_ref, top_ref, total_ref):
    pairs = q_ref.shape[0]
    span = kv_ref.shape[2]
    lane = lax.broadcasted_iota(jnp.int32, (2 * GROUP, 2 * span), 1)
    second = lax.broadcasted_iota(jnp.int32, (2 * GROUP, 2 * span), 0) >= GROUP
    first_lane = jnp.where(second, span, 0)

    def one_pair(p):
        keys = kv_ref[pl.ds(2 * p, 2), 0].reshape(2 * span, HD)
        values = kv_ref[pl.ds(2 * p, 2), 1].reshape(2 * span, HD)
        scores = (
            lax.dot_general(q_ref[p], keys, NT, preferred_element_type=jnp.float32)
            * SCORE_SCALE
        )
        end_lane = first_lane + jnp.where(second, length_ref[2 * p + 1], length_ref[2 * p])
        live = (lane >= first_lane) & (lane < end_lane)
        top = jnp.max(jnp.where(live, scores, -jnp.inf), axis=-1, keepdims=True)
        weights = jnp.where(live, jnp.exp2(scores - top), 0.0)
        total = jnp.sum(weights, axis=-1, keepdims=True)
        weighted = jnp.dot(
            weights.astype(jnp.bfloat16), values, preferred_element_type=jnp.float32
        )
        shape = (2, GROUP, HD)
        sum_ref[pl.ds(2 * p, 2)] = weighted.reshape(shape)
        top_ref[pl.ds(2 * p, 2)] = jnp.broadcast_to(top, (2 * GROUP, HD)).reshape(shape)
        total_ref[pl.ds(2 * p, 2)] = jnp.broadcast_to(total, (2 * GROUP, HD)).reshape(shape)

    step = 8

    def body(s, carry):
        for u in range(step):
            one_pair(s * step + u)
        return carry

    lax.fori_loop(0, pairs // step, body, 0)


def suffix_attend(lengths, q_home, kv):
    count = lengths.shape[0]
    span = kv.shape[2]
    out = jax.ShapeDtypeStruct((count, GROUP, HD), jnp.float32)
    vmem = pl.BlockSpec(memory_space=pltpu.VMEM)
    return pl.pallas_call(
        suffix_kernel,
        out_shape=(out, out, out),
        in_specs=[pl.BlockSpec(memory_space=pltpu.SMEM), vmem, vmem],
        out_specs=(vmem, vmem, vmem),
        cost_estimate=pl.CostEstimate(
            flops=4 * count * GROUP * span * HD,
            bytes_accessed=kv.size * 2,
            transcendentals=count * GROUP * span,
        ),
        compiler_params=pltpu.CompilerParams(vmem_limit_bytes=12 << 20),
        name="suffix_attend",
    )(lengths, q_home, kv)


def prefix_kernel(q_ref, k_ref, v_ref, main_ref, stat_ref, s0_ref, s1_ref, m0_ref, m1_ref):
    rows = q_ref.shape[0]
    span = k_ref.shape[0]
    blocks = rows // BLOCK
    chunks = span // CHUNK
    per_home = SLOTS * GROUP
    homes = BLOCK // per_home

    def stage(ahead, s_ahead, m_ahead, now, s_now, m_now):
        if ahead is not None:
            q = q_ref[pl.ds(pl.multiple_of(ahead * BLOCK, BLOCK), BLOCK), :]
            top = jnp.full((BLOCK, HD), -jnp.inf, jnp.float32)
        if now is not None:
            shift = m_now[...]
            total = jnp.zeros((BLOCK, HD), jnp.float32)
            weighted = jnp.zeros((BLOCK, HD), jnp.float32)
        for c in range(chunks):
            at = c * CHUNK
            if ahead is not None:
                scores = lax.dot_general(
                    q, k_ref[at : at + CHUNK, :], NT, preferred_element_type=jnp.float32
                )
                s_ahead[:, at : at + CHUNK] = scores
                for l in range(0, CHUNK, HD):
                    top = jnp.maximum(top, scores[:, l : l + HD])
            if now is not None:
                parts = []
                for l in range(at, at + CHUNK, HD):
                    w = jnp.exp2(s_now[:, l : l + HD] * SCORE_SCALE - shift)
                    total = total + w
                    parts.append(w.astype(jnp.bfloat16))
                weighted = weighted + jnp.dot(
                    jnp.concatenate(parts, axis=1),
                    v_ref[at : at + CHUNK, :],
                    preferred_element_type=jnp.float32,
                )
        if ahead is not None:
            m_ahead[...] = jnp.broadcast_to(
                jnp.max(top, axis=-1, keepdims=True) * SCORE_SCALE, (BLOCK, HD)
            )
        if now is not None:
            mass = jnp.sum(total, axis=-1, keepdims=True)
            part = weighted / mass
            largest = jnp.max(jnp.abs(part), axis=-1, keepdims=True)
            step = jnp.ceil(jnp.log2(jnp.maximum(largest, 1e-30)) * 8.0)
            code = jnp.round(part * (jnp.exp2(step * -0.125) * CODE_TOP))
            code = jnp.clip(code, -CODE_TOP, CODE_TOP)
            start = pl.multiple_of(now * BLOCK, BLOCK)
            main_ref[pl.ds(start, BLOCK), :] = code.astype(jnp.int32).astype(jnp.int16)
            lse = shift[:, :1] + jnp.log2(mass)
            coarse = jnp.round(lse * 4.0)
            fine = jnp.round((lse - coarse * 0.25) * 131072.0)
            lane = lax.broadcasted_iota(jnp.int32, (BLOCK, HD), 1)
            inner = lax.broadcasted_iota(jnp.int32, (BLOCK, HD), 0) % per_home
            upper = jnp.where(lane == inner, coarse, 0.0) + jnp.where(
                lane == inner + per_home, step, 0.0
            )
            lower = jnp.where(lane == inner, fine, 0.0)
            upper = jnp.sum(upper.reshape(homes, per_home, HD), axis=1)
            lower = jnp.sum(lower.reshape(homes, per_home, HD), axis=1)
            first = pl.multiple_of(now * homes, homes)
            stat_ref[0, pl.ds(first, homes), :] = upper
            stat_ref[1, pl.ds(first, homes), :] = lower

    stage(0, s0_ref, m0_ref, None, None, None)

    def body(i, carry):
        stage(2 * i + 1, s1_ref, m1_ref, 2 * i, s0_ref, m0_ref)
        stage(2 * i + 2, s0_ref, m0_ref, 2 * i + 1, s1_ref, m1_ref)
        return carry

    lax.fori_loop(0, blocks // 2 - 1, body, 0)
    stage(blocks - 1, s1_ref, m1_ref, blocks - 2, s0_ref, m0_ref)
    stage(None, None, None, blocks - 1, s1_ref, m1_ref)


def prefix_attend(q_slots, prefix_kv):
    rows = q_slots.shape[0]
    span = prefix_kv.shape[3]
    homes = rows // (SLOTS * GROUP)
    whole = lambda *shape: pl.BlockSpec(shape, lambda i: (0,) * len(shape))
    return pl.pallas_call(
        prefix_kernel,
        grid=(1,),
        out_shape=(
            jax.ShapeDtypeStruct((rows, HD), jnp.int16),
            jax.ShapeDtypeStruct((2, homes, HD), jnp.float32),
        ),
        in_specs=[
            whole(rows, HD),
            pl.BlockSpec((None, None, None, span, HD), lambda i: (0, 0, 0, 0, 0)),
            pl.BlockSpec((None, None, None, span, HD), lambda i: (0, 1, 0, 0, 0)),
        ],
        out_specs=(whole(rows, HD), whole(2, homes, HD)),
        scratch_shapes=[
            pltpu.VMEM((BLOCK, span), jnp.float32),
            pltpu.VMEM((BLOCK, span), jnp.float32),
            pltpu.VMEM((BLOCK, HD), jnp.float32),
            pltpu.VMEM((BLOCK, HD), jnp.float32),
        ],
        cost_estimate=pl.CostEstimate(
            flops=4 * rows * span * HD,
            bytes_accessed=prefix_kv.size * 2,
            transcendentals=rows * span,
        ),
        compiler_params=pltpu.CompilerParams(vmem_limit_bytes=24 << 20),
        name="prefix_attend",
    )(q_slots, prefix_kv, prefix_kv)


def combine_kernel(slot_ref, main_ref, stat_ref, sum_ref, top_ref, total_ref, out_ref, tile_ref):
    tensor, rows, width = out_ref.shape
    lane = lax.broadcasted_iota(jnp.int32, (GROUP, HD), 1)
    head = lax.broadcasted_iota(jnp.int32, (GROUP, HD), 0)
    for t in range(tensor):
        for i in range(rows):
            r = t * rows + i
            slot = slot_ref[r]
            stats = jnp.broadcast_to(stat_ref[pl.ds(slot // SLOTS, 1), :], (GROUP, HD))
            at = head + (slot % SLOTS) * GROUP
            lse = jnp.sum(jnp.where(lane == at, stats, 0.0), axis=-1, keepdims=True)
            scale = jnp.sum(
                jnp.where(lane == at + SLOTS * GROUP, stats, 0.0), axis=-1, keepdims=True
            )
            part = main_ref[slot].astype(jnp.int32).astype(jnp.float32) * scale
            top = top_ref[r]
            joint = jnp.maximum(top, lse)
            prefix_mass = jnp.exp2(lse - joint)
            suffix_mass = jnp.exp2(top - joint)
            result = (prefix_mass * part + suffix_mass * sum_ref[r]) / (
                prefix_mass + suffix_mass * total_ref[r]
            )
            tile_ref[pl.ds(t * GROUP * rows + i, GROUP, stride=rows), :] = result
        for h in range(GROUP):
            out_ref[t, :, h * HD : (h + 1) * HD] = tile_ref[
                pl.ds((t * GROUP + h) * rows, rows), :
            ].astype(jnp.bfloat16)


def combine(slot, main, stats, suffix, tensor):
    count = slot.shape[0]
    vmem = pl.BlockSpec(memory_space=pltpu.VMEM)
    return pl.pallas_call(
        combine_kernel,
        out_shape=jax.ShapeDtypeStruct((tensor, count // tensor, GROUP * HD), jnp.bfloat16),
        in_specs=[pl.BlockSpec(memory_space=pltpu.SMEM)] + [vmem] * 5,
        out_specs=vmem,
        scratch_shapes=[pltpu.VMEM((count * GROUP, HD), jnp.float32)],
        compiler_params=pltpu.CompilerParams(vmem_limit_bytes=8 << 20),
        name="combine",
    )(slot, main, stats, *suffix)


def on_device(queries, suffix_kv, suffix_lengths, prefix_kv, tree_ids, owner_map):
    owners = lax.axis_size("prefix")
    tensor = lax.axis_size("tensor")
    rows = queries.shape[0]
    count = tree_ids.shape[0]
    width = GROUP * HD
    local_q = lax.all_to_all(queries, "tensor", split_axis=1, concat_axis=0, tiled=True)
    q_rows = local_q.reshape(tensor, rows, width)

    prompt = jnp.arange(owner_map.shape[0], dtype=jnp.int32)
    owner_row = jnp.sum(jnp.where(tree_ids[:, None] == prompt[None, :], owner_map[None, :], 0), axis=1)
    place = jnp.arange(count, dtype=jnp.int32)
    earlier = (tree_ids[:, None] == tree_ids[None, :]) & (place[None, :] < place[:, None])
    slot = owner_row * SLOTS + jnp.sum(earlier.astype(jnp.int32), axis=1)

    outgoing, q_home = dispatch(slot, q_rows)
    arrived = lax.all_to_all(
        outgoing.reshape(owners, SLOTS * GROUP, HD), "prefix", split_axis=0, concat_axis=0, tiled=True
    )
    suffix = suffix_attend(suffix_lengths, q_home, suffix_kv[:, :, 0])
    main, stats = prefix_attend(arrived.reshape(owners * SLOTS * GROUP, HD), prefix_kv)
    pairs = SLOTS * GROUP // 2
    stats = jnp.swapaxes(stats, 0, 1).astype(jnp.int16).reshape(owners, 1, 2, HD)
    sent = jnp.concatenate([main.reshape(owners, pairs, 2, HD), stats], axis=1)
    back = lax.all_to_all(sent, "prefix", split_axis=0, concat_axis=0, tiled=True)
    back_main = back[:, :pairs].reshape(owners * SLOTS, GROUP, HD)
    upper = back[:, pairs, 0].astype(jnp.float32)
    lower = back[:, pairs, 1].astype(jnp.float32)
    lane = lax.broadcasted_iota(jnp.int32, (owners, HD), 1)
    back_stats = jnp.where(
        lane < SLOTS * GROUP,
        upper * 0.25 + lower * (1.0 / 131072.0),
        jnp.exp2(upper * 0.125) * (1.0 / CODE_TOP),
    )
    attended = combine(slot, back_main, back_stats, suffix, tensor)
    done = lax.all_to_all(attended, "tensor", split_axis=0, concat_axis=0, tiled=True)
    return jnp.swapaxes(done, 0, 1).reshape(rows, tensor * width)


def solution(mesh):
    in_specs = (
        P(("prefix", "tensor"), None),
        P("prefix", None, "tensor", None, None),
        P("prefix"),
        P("prefix", None, "tensor", None, None),
        P("prefix"),
        P(),
    )
    out_specs = P(("prefix", "tensor"), None)
    return jax.shard_map(
        on_device, mesh=mesh, in_specs=in_specs, out_specs=out_specs, check_vma=False
    )
```

```python
import math

import jax
import jax.numpy as jnp
from jax import lax
from jax.experimental import pallas as pl
from jax.experimental.pallas import tpu as pltpu
from jax.sharding import PartitionSpec as P

H = 64
KVH = 8
HD = 128
GROUP = H // KVH
SLOTS = 2
CODE_TOP = 32767.0
SCORE_SCALE = math.log2(math.e) / math.sqrt(HD)

BLOCK = 256
CHUNK = 256
PAIRS = 8
PAIR = SLOTS * GROUP
SENT = PAIR + 2

NT = (((1,), (1,)), ((), ()))


def dispatch_kernel(slot_ref, q_ref, out_ref, home_ref, tile_ref):
    tensor, rows, width = q_ref.shape
    for t in range(tensor):
        for h in range(GROUP):
            tile_ref[pl.ds((t * GROUP + h) * rows, rows), :] = q_ref[
                t, :, h * HD : (h + 1) * HD
            ].astype(jnp.float32)
    for r in range(0, tensor * rows, 2):
        pair = []
        for k in range(2):
            t, i = divmod(r + k, rows)
            tile = tile_ref[pl.ds(t * GROUP * rows + i, GROUP, stride=rows), :]
            pair.append(tile)
            out_ref[slot_ref[r + k]] = tile.astype(jnp.bfloat16)
        home_ref[r // 2] = jnp.concatenate(pair, axis=0).astype(jnp.bfloat16)


def dispatch(slot, q_rows):
    tensor, rows, width = q_rows.shape
    count = tensor * rows
    owners = count
    return pl.pallas_call(
        dispatch_kernel,
        out_shape=(
            jax.ShapeDtypeStruct((owners * SLOTS, GROUP, HD), jnp.bfloat16),
            jax.ShapeDtypeStruct((count // 2, 2 * GROUP, HD), jnp.bfloat16),
        ),
        in_specs=[
            pl.BlockSpec(memory_space=pltpu.SMEM),
            pl.BlockSpec(memory_space=pltpu.VMEM),
        ],
        out_specs=(
            pl.BlockSpec(memory_space=pltpu.VMEM),
            pl.BlockSpec(memory_space=pltpu.VMEM),
        ),
        scratch_shapes=[pltpu.VMEM((count * GROUP, HD), jnp.float32)],
        compiler_params=pltpu.CompilerParams(vmem_limit_bytes=8 << 20),
        name="dispatch",
    )(slot, q_rows)


def suffix_kernel(length_ref, q_ref, kv_ref, prefix_ref, part_ref, lse_ref, keys_ref, turned_ref):
    pairs = q_ref.shape[0]
    span = kv_ref.shape[2]
    lane = lax.broadcasted_iota(jnp.int32, (2 * GROUP, 2 * span), 1)
    second = lax.broadcasted_iota(jnp.int32, (2 * GROUP, 2 * span), 0) >= GROUP
    first_lane = jnp.where(second, span, 0)

    def some_pairs(first):
        scores, live = [], []
        for u in range(PAIRS):
            p = first + u
            keys = kv_ref[pl.ds(2 * p, 2), 0].reshape(2 * span, HD)
            scores.append(
                lax.dot_general(q_ref[p], keys, NT, preferred_element_type=jnp.float32)
            )
            end_lane = first_lane + jnp.where(second, length_ref[2 * p + 1], length_ref[2 * p])
            live.append((lane >= first_lane) & (lane < end_lane))
        masked = [
            jnp.where(m, x * SCORE_SCALE, -jnp.inf) for m, x in zip(live, scores)
        ]
        tops = [jnp.max(x, axis=-1, keepdims=True) for x in masked]
        weights = [jnp.exp2(x - t) for x, t in zip(masked, tops)]
        totals = [jnp.sum(w, axis=-1, keepdims=True) for w in weights]
        sums = []
        for u in range(PAIRS):
            values = kv_ref[pl.ds(2 * (first + u), 2), 1].reshape(2 * span, HD)
            sums.append(
                jnp.dot(
                    weights[u].astype(jnp.bfloat16), values, preferred_element_type=jnp.float32
                )
            )
        shape = (2, GROUP, HD)
        for u in range(PAIRS):
            at = pl.ds(2 * (first + u), 2)
            part_ref[at] = (sums[u] / totals[u]).reshape(shape)
            lse = tops[u] + jnp.log2(totals[u])
            lse_ref[at] = jnp.broadcast_to(lse, (2 * GROUP, HD)).reshape(shape)

    def body(s, carry):
        some_pairs(s * PAIRS)
        return carry

    lax.fori_loop(0, pairs // PAIRS, body, 0)
    keys_ref[...] = prefix_ref[0, 0, 0]
    for at in range(0, prefix_ref.shape[3], 2 * HD):
        turned_ref[:, at : at + 2 * HD] = prefix_ref[0, 1, 0, at : at + 2 * HD, :].T


def suffix_attend(lengths, q_home, kv, prefix_kv):
    count = lengths.shape[0]
    span = kv.shape[2]
    out = jax.ShapeDtypeStruct((count, GROUP, HD), jnp.float32)
    vmem = pl.BlockSpec(memory_space=pltpu.VMEM)
    return pl.pallas_call(
        suffix_kernel,
        out_shape=(out, out, jax.ShapeDtypeStruct((prefix_kv.shape[3], HD), jnp.bfloat16), jax.ShapeDtypeStruct((HD, prefix_kv.shape[3]), jnp.bfloat16)),
        in_specs=[pl.BlockSpec(memory_space=pltpu.SMEM), vmem, vmem, vmem],
        out_specs=(vmem, vmem, vmem, vmem),
        cost_estimate=pl.CostEstimate(
            flops=4 * count * GROUP * span * HD,
            bytes_accessed=(kv.size + prefix_kv.size) * 2,
            transcendentals=count * GROUP * span,
        ),
        compiler_params=pltpu.CompilerParams(vmem_limit_bytes=16 << 20),
        name="suffix_attend",
    )(lengths, q_home, kv, prefix_kv)


def prefix_kernel(
    q_ref, k_ref, vt_ref, sent_ref, s0_ref, s1_ref, m0_ref, m1_ref
):
    rows = q_ref.shape[0]
    span = k_ref.shape[0]
    blocks = rows // BLOCK
    chunks = span // CHUNK
    homes = HD // PAIR

    def fold(x, op):
        return op(x.reshape(CHUNK // 8, 8, BLOCK), axis=0)

    def finish(now, weighted, mass, shift):
        part = weighted / mass
        largest = jnp.max(jnp.abs(part), axis=0, keepdims=True)
        step = jnp.ceil(jnp.log2(jnp.maximum(largest, 1e-30)) * 8.0)
        code = jnp.round(part * (jnp.exp2(step * -0.125) * CODE_TOP))
        code = jnp.clip(code, -CODE_TOP, CODE_TOP)
        lse = shift + jnp.log2(mass)
        coarse = jnp.round(lse * 4.0)
        fine = jnp.round((lse - coarse * 0.25) * 131072.0)
        lane = lax.broadcasted_iota(jnp.int32, (homes, HD), 1)
        home = lax.broadcasted_iota(jnp.int32, (homes, HD), 0)
        mine = lane // PAIR == home
        other = ((lane + HD // 2) % HD) // PAIR == home
        for g in range(BLOCK // HD):
            cut = slice(g * HD, (g + 1) * HD)
            rows_code = code[:, cut].T
            wide = lambda x: jnp.broadcast_to(x, (homes, HD))
            upper = jnp.where(mine, wide(coarse[:, cut]), 0.0)
            turned = pltpu.roll(wide(step[:, cut]), HD // 2, 1)
            upper = upper + jnp.where(other, turned, 0.0)
            lower = jnp.where(mine, wide(fine[:, cut]), 0.0)
            pieces = []
            for u in range(homes):
                pieces += [
                    rows_code[u * PAIR : (u + 1) * PAIR],
                    upper[u : u + 1],
                    lower[u : u + 1],
                ]
            packed = jnp.concatenate(pieces, axis=0).astype(jnp.int32).astype(jnp.int16)
            size = homes * SENT
            start = pl.multiple_of((now * (BLOCK // HD) + g) * size, size)
            sent_ref[pl.ds(start, size), :] = packed

    def stage(ahead, s_ahead, m_ahead, now, s_now, m_now):
        if ahead is not None:
            q = q_ref[pl.ds(pl.multiple_of(ahead * BLOCK, BLOCK), BLOCK), :]
            top = jnp.full((8, BLOCK), -jnp.inf, jnp.float32)
        if now is not None:
            shift = m_now[0:1, :]
            total = jnp.zeros((8, BLOCK), jnp.float32)
            weighted = jnp.zeros((HD, BLOCK), jnp.float32)
        for c in range(chunks):
            at = c * CHUNK
            if ahead is not None:
                scores = lax.dot_general(
                    k_ref[at : at + CHUNK, :], q, NT, preferred_element_type=jnp.float32
                )
                s_ahead[at : at + CHUNK, :] = scores
                top = jnp.maximum(top, fold(scores, jnp.max))
            if now is not None:
                w = jnp.exp2(s_now[at : at + CHUNK, :] * SCORE_SCALE - shift)
                total = total + fold(w, jnp.sum)
                weighted = weighted + jnp.dot(
                    vt_ref[:, at : at + CHUNK],
                    w.astype(jnp.bfloat16),
                    preferred_element_type=jnp.float32,
                )
        if ahead is not None:
            m_ahead[...] = jnp.broadcast_to(
                jnp.max(top, axis=0, keepdims=True) * SCORE_SCALE, (8, BLOCK)
            )
        if now is not None:
            finish(now, weighted, jnp.sum(total, axis=0, keepdims=True), shift)

    stage(0, s0_ref, m0_ref, None, None, None)
    for b in range(blocks - 1):
        even, odd = (s0_ref, m0_ref), (s1_ref, m1_ref)
        if b % 2 == 0:
            stage(b + 1, *odd, b, *even)
        else:
            stage(b + 1, *even, b, *odd)
    stage(None, None, None, blocks - 1, s1_ref, m1_ref)


def prefix_attend(q_slots, keys, values_t):
    rows = q_slots.shape[0]
    span = keys.shape[0]
    homes = rows // PAIR
    vmem = pl.BlockSpec(memory_space=pltpu.VMEM)
    return pl.pallas_call(
        prefix_kernel,
        out_shape=jax.ShapeDtypeStruct((homes * SENT, HD), jnp.int16),
        in_specs=[vmem] * 3,
        out_specs=vmem,
        scratch_shapes=[
            pltpu.VMEM((span, BLOCK), jnp.float32),
            pltpu.VMEM((span, BLOCK), jnp.float32),
            pltpu.VMEM((8, BLOCK), jnp.float32),
            pltpu.VMEM((8, BLOCK), jnp.float32),
        ],
        cost_estimate=pl.CostEstimate(
            flops=4 * rows * span * HD,
            bytes_accessed=keys.size * 4,
            transcendentals=rows * span,
        ),
        compiler_params=pltpu.CompilerParams(vmem_limit_bytes=24 << 20),
        name="prefix_attend",
    )(q_slots, keys, values_t)


def combine_kernel(
    slot_ref, back_ref, part_ref, lse_ref, out_ref, back32_ref, tile_ref
):
    tensor, rows, width = out_ref.shape
    lane = lax.broadcasted_iota(jnp.int32, (GROUP, HD), 1)
    head = lax.broadcasted_iota(jnp.int32, (GROUP, HD), 0)
    own = (slot_ref[tensor * rows] % (HD // PAIR)) * PAIR
    own_step = (own + HD // 2) % HD
    for k in range(0, back_ref.shape[0], 16):
        back32_ref[k : k + 16, :] = back_ref[k : k + 16, :].astype(jnp.int32).astype(jnp.float32)
    for t in range(tensor):
        for i in range(rows):
            r = t * rows + i
            slot = slot_ref[r]
            base = (slot // SLOTS) * SENT
            inner = (slot % SLOTS) * GROUP
            upper = back32_ref[pl.ds(base + PAIR, 1), :]
            lower = back32_ref[pl.ds(base + PAIR + 1, 1), :]
            at = head + inner

            def pick(row, where):
                wide = jnp.broadcast_to(row, (GROUP, HD))
                return jnp.sum(jnp.where(lane == where, wide, 0.0), axis=-1, keepdims=True)

            lse = pick(upper * 0.25 + lower * (1.0 / 131072.0), at + own)
            step = pick(upper, at + own_step)
            scale = jnp.exp2(step * 0.125) * (1.0 / CODE_TOP)
            part = back32_ref[pl.ds(base + inner, GROUP), :] * scale
            suffix_lse = lse_ref[r]
            joint = jnp.maximum(suffix_lse, lse)
            prefix_mass = jnp.exp2(lse - joint)
            suffix_mass = jnp.exp2(suffix_lse - joint)
            result = (prefix_mass * part + suffix_mass * part_ref[r]) / (
                prefix_mass + suffix_mass
            )
            tile_ref[pl.ds(t * GROUP * rows + i, GROUP, stride=rows), :] = result
        for h in range(GROUP):
            out_ref[t, :, h * HD : (h + 1) * HD] = tile_ref[
                pl.ds((t * GROUP + h) * rows, rows), :
            ].astype(jnp.bfloat16)


def combine(slot, back, suffix, tensor):
    count = slot.shape[0] - 1
    vmem = pl.BlockSpec(memory_space=pltpu.VMEM)
    smem = pl.BlockSpec(memory_space=pltpu.SMEM)
    return pl.pallas_call(
        combine_kernel,
        out_shape=jax.ShapeDtypeStruct((tensor, count // tensor, GROUP * HD), jnp.bfloat16),
        in_specs=[smem] + [vmem] * 3,
        out_specs=vmem,
        scratch_shapes=[
            pltpu.VMEM(back.shape, jnp.float32),
            pltpu.VMEM((count * GROUP, HD), jnp.float32),
        ],
        compiler_params=pltpu.CompilerParams(vmem_limit_bytes=8 << 20),
        name="combine",
    )(slot, back, *suffix)


def on_device(queries, suffix_kv, suffix_lengths, prefix_kv, tree_ids, owner_map):
    owners = lax.axis_size("prefix")
    tensor = lax.axis_size("tensor")
    rows = queries.shape[0]
    count = tree_ids.shape[0]
    width = GROUP * HD
    local_q = lax.all_to_all(queries, "tensor", split_axis=1, concat_axis=0, tiled=True)
    q_rows = local_q.reshape(tensor, rows, width)

    prompt = jnp.arange(owner_map.shape[0], dtype=jnp.int32)
    owner_row = jnp.sum(jnp.where(tree_ids[:, None] == prompt[None, :], owner_map[None, :], 0), axis=1)
    place = jnp.arange(count, dtype=jnp.int32)
    earlier = (tree_ids[:, None] == tree_ids[None, :]) & (place[None, :] < place[:, None])
    slot = owner_row * SLOTS + jnp.sum(earlier.astype(jnp.int32), axis=1)

    home = lax.axis_index("prefix").astype(jnp.int32)
    slot = jnp.concatenate([slot, home.reshape(1)])
    outgoing, q_home = dispatch(slot, q_rows)
    arrived = lax.all_to_all(
        outgoing.reshape(owners, SLOTS * GROUP, HD), "prefix", split_axis=0, concat_axis=0, tiled=True
    )
    *suffix, keys, values_t = suffix_attend(suffix_lengths, q_home, suffix_kv[:, :, 0], prefix_kv)
    packed = prefix_attend(arrived.reshape(owners * PAIR, HD), keys, values_t)
    back = lax.all_to_all(
        packed.reshape(owners, SENT // 2, 2, HD), "prefix", split_axis=0, concat_axis=0, tiled=True
    )
    attended = combine(slot, back.reshape(owners * SENT, HD), suffix, tensor)
    done = lax.all_to_all(attended, "tensor", split_axis=0, concat_axis=0, tiled=True)
    return jnp.swapaxes(done, 0, 1).reshape(rows, tensor * width)


def solution(mesh):
    in_specs = (
        P(("prefix", "tensor"), None),
        P("prefix", None, "tensor", None, None),
        P("prefix"),
        P("prefix", None, "tensor", None, None),
        P("prefix"),
        P(),
    )
    out_specs = P(("prefix", "tensor"), None)
    return jax.shard_map(
        on_device, mesh=mesh, in_specs=in_specs, out_specs=out_specs, check_vma=False
    )
```

```python
import math

import jax
import jax.numpy as jnp
from jax import lax
from jax.experimental import pallas as pl
from jax.experimental.pallas import tpu as pltpu
from jax.sharding import PartitionSpec as P

H = 64
KVH = 8
HD = 128
GROUP = H // KVH
SLOTS = 2
CODE_TOP = 32767.0
SCORE_SCALE = math.log2(math.e) / math.sqrt(HD)

BLOCK = 256
CHUNK = 1024
PAIRS = 8
PAIR = SLOTS * GROUP
SENT = PAIR + 2

NT = (((1,), (1,)), ((), ()))


def dispatch_kernel(slot_ref, q_ref, out_ref, home_ref, tile_ref):
    tensor, rows, width = q_ref.shape
    for t in range(tensor):
        for h in range(GROUP):
            tile_ref[pl.ds((t * GROUP + h) * rows, rows), :] = q_ref[
                t, :, h * HD : (h + 1) * HD
            ].astype(jnp.float32)
    for r in range(0, tensor * rows, 2):
        pair = []
        for k in range(2):
            t, i = divmod(r + k, rows)
            tile = tile_ref[pl.ds(t * GROUP * rows + i, GROUP, stride=rows), :]
            pair.append(tile)
            out_ref[slot_ref[r + k]] = tile.astype(jnp.bfloat16)
        home_ref[r // 2] = jnp.concatenate(pair, axis=0).astype(jnp.bfloat16)


def dispatch(slot, q_rows):
    tensor, rows, width = q_rows.shape
    count = tensor * rows
    owners = count
    return pl.pallas_call(
        dispatch_kernel,
        out_shape=(
            jax.ShapeDtypeStruct((owners * SLOTS, GROUP, HD), jnp.bfloat16),
            jax.ShapeDtypeStruct((count // 2, 2 * GROUP, HD), jnp.bfloat16),
        ),
        in_specs=[
            pl.BlockSpec(memory_space=pltpu.SMEM),
            pl.BlockSpec(memory_space=pltpu.VMEM),
        ],
        out_specs=(
            pl.BlockSpec(memory_space=pltpu.VMEM),
            pl.BlockSpec(memory_space=pltpu.VMEM),
        ),
        scratch_shapes=[pltpu.VMEM((count * GROUP, HD), jnp.float32)],
        compiler_params=pltpu.CompilerParams(vmem_limit_bytes=8 << 20),
        name="dispatch",
    )(slot, q_rows)


def suffix_kernel(length_ref, q_ref, kv_ref, prefix_ref, part_ref, lse_ref, keys_ref, turned_ref):
    pairs = q_ref.shape[0]
    span = kv_ref.shape[2]
    lane = lax.broadcasted_iota(jnp.int32, (2 * GROUP, 2 * span), 1)
    second = lax.broadcasted_iota(jnp.int32, (2 * GROUP, 2 * span), 0) >= GROUP
    first_lane = jnp.where(second, span, 0)

    def some_pairs(first):
        scores, live = [], []
        for u in range(PAIRS):
            p = first + u
            keys = kv_ref[pl.ds(2 * p, 2), 0].reshape(2 * span, HD)
            scores.append(
                lax.dot_general(q_ref[p], keys, NT, preferred_element_type=jnp.float32)
            )
            end_lane = first_lane + jnp.where(second, length_ref[2 * p + 1], length_ref[2 * p])
            live.append((lane >= first_lane) & (lane < end_lane))
        masked = [
            jnp.where(m, x * SCORE_SCALE, -jnp.inf) for m, x in zip(live, scores)
        ]
        tops = [jnp.max(x, axis=-1, keepdims=True) for x in masked]
        weights = [jnp.exp2(x - t) for x, t in zip(masked, tops)]
        totals = [jnp.sum(w, axis=-1, keepdims=True) for w in weights]
        sums = []
        for u in range(PAIRS):
            values = kv_ref[pl.ds(2 * (first + u), 2), 1].reshape(2 * span, HD)
            sums.append(
                jnp.dot(
                    weights[u].astype(jnp.bfloat16), values, preferred_element_type=jnp.float32
                )
            )
        shape = (2, GROUP, HD)
        for u in range(PAIRS):
            at = pl.ds(2 * (first + u), 2)
            part_ref[at] = (sums[u] / totals[u]).reshape(shape)
            lse = tops[u] + jnp.log2(totals[u])
            lse_ref[at] = jnp.broadcast_to(lse, (2 * GROUP, HD)).reshape(shape)

    def body(s, carry):
        some_pairs(s * PAIRS)
        return carry

    lax.fori_loop(0, pairs // PAIRS, body, 0)
    keys_ref[...] = prefix_ref[0, 0, 0]
    for k in range(turned_ref.shape[0]):
        turned_ref[k] = prefix_ref[0, 1, 0, k * HD : (k + 1) * HD, :].T


def suffix_attend(lengths, q_home, kv, prefix_kv):
    count = lengths.shape[0]
    span = kv.shape[2]
    out = jax.ShapeDtypeStruct((count, GROUP, HD), jnp.float32)
    vmem = pl.BlockSpec(memory_space=pltpu.VMEM)
    return pl.pallas_call(
        suffix_kernel,
        out_shape=(out, out, jax.ShapeDtypeStruct((prefix_kv.shape[3], HD), jnp.bfloat16), jax.ShapeDtypeStruct((prefix_kv.shape[3] // HD, HD, HD), jnp.bfloat16)),
        in_specs=[pl.BlockSpec(memory_space=pltpu.SMEM), vmem, vmem, vmem],
        out_specs=(vmem, vmem, vmem, vmem),
        cost_estimate=pl.CostEstimate(
            flops=4 * count * GROUP * span * HD,
            bytes_accessed=(kv.size + prefix_kv.size) * 2,
            transcendentals=count * GROUP * span,
        ),
        compiler_params=pltpu.CompilerParams(vmem_limit_bytes=16 << 20),
        name="suffix_attend",
    )(lengths, q_home, kv, prefix_kv)


def prefix_kernel(
    q_ref, k_ref, vt_ref, sent_ref, s0_ref, s1_ref, m0_ref, m1_ref
):
    rows = q_ref.shape[0]
    span = k_ref.shape[0]
    blocks = rows // BLOCK
    chunks = span // CHUNK
    homes = HD // PAIR

    def turned(at):
        tiles = [vt_ref[k] for k in range(at // HD, (at + CHUNK) // HD)]
        return jnp.concatenate(tiles, axis=1)

    def fold(x, op):
        return op(x.reshape(CHUNK // 8, 8, BLOCK), axis=0)

    def finish(now, weighted, mass, shift):
        part = weighted / mass
        largest = jnp.max(jnp.abs(part), axis=0, keepdims=True)
        step = jnp.ceil(jnp.log2(jnp.maximum(largest, 1e-30)) * 8.0)
        code = jnp.round(part * (jnp.exp2(step * -0.125) * CODE_TOP))
        code = jnp.clip(code, -CODE_TOP, CODE_TOP)
        lse = shift + jnp.log2(mass)
        coarse = jnp.round(lse * 4.0)
        fine = jnp.round((lse - coarse * 0.25) * 131072.0)
        lane = lax.broadcasted_iota(jnp.int32, (homes, HD), 1)
        home = lax.broadcasted_iota(jnp.int32, (homes, HD), 0)
        mine = lane // PAIR == home
        other = ((lane + HD // 2) % HD) // PAIR == home
        for g in range(BLOCK // HD):
            cut = slice(g * HD, (g + 1) * HD)
            rows_code = code[:, cut].T
            wide = lambda x: jnp.broadcast_to(x, (homes, HD))
            upper = jnp.where(mine, wide(coarse[:, cut]), 0.0)
            turned = pltpu.roll(wide(step[:, cut]), HD // 2, 1)
            upper = upper + jnp.where(other, turned, 0.0)
            lower = jnp.where(mine, wide(fine[:, cut]), 0.0)
            pieces = []
            for u in range(homes):
                pieces += [
                    rows_code[u * PAIR : (u + 1) * PAIR],
                    upper[u : u + 1],
                    lower[u : u + 1],
                ]
            packed = jnp.concatenate(pieces, axis=0).astype(jnp.int32).astype(jnp.int16)
            size = homes * SENT
            start = pl.multiple_of((now * (BLOCK // HD) + g) * size, size)
            sent_ref[pl.ds(start, size), :] = packed

    def stage(ahead, s_ahead, m_ahead, now, s_now, m_now):
        if ahead is not None:
            q = q_ref[pl.ds(pl.multiple_of(ahead * BLOCK, BLOCK), BLOCK), :]
            top = jnp.full((8, BLOCK), -jnp.inf, jnp.float32)
        if now is not None:
            shift = m_now[0:1, :]
            total = jnp.zeros((8, BLOCK), jnp.float32)
            weighted = [jnp.zeros((HD, BLOCK), jnp.float32)] * 2
        for c in range(chunks):
            at = c * CHUNK
            if ahead is not None:
                scores = lax.dot_general(
                    k_ref[at : at + CHUNK, :], q, NT, preferred_element_type=jnp.float32
                )
                s_ahead[at : at + CHUNK, :] = scores
                top = jnp.maximum(top, fold(scores, jnp.max))
            if now is not None:
                w = jnp.exp2(s_now[at : at + CHUNK, :] * SCORE_SCALE - shift)
                total = total + fold(w, jnp.sum)
                weighted[c % 2] = weighted[c % 2] + jnp.dot(
                    turned(at),
                    w.astype(jnp.bfloat16),
                    preferred_element_type=jnp.float32,
                )
        if ahead is not None:
            m_ahead[...] = jnp.broadcast_to(
                jnp.max(top, axis=0, keepdims=True) * SCORE_SCALE, (8, BLOCK)
            )
        if now is not None:
            finish(now, weighted[0] + weighted[1], jnp.sum(total, axis=0, keepdims=True), shift)

    stage(0, s0_ref, m0_ref, None, None, None)
    for b in range(blocks - 1):
        even, odd = (s0_ref, m0_ref), (s1_ref, m1_ref)
        if b % 2 == 0:
            stage(b + 1, *odd, b, *even)
        else:
            stage(b + 1, *even, b, *odd)
    stage(None, None, None, blocks - 1, s1_ref, m1_ref)


def prefix_attend(q_slots, keys, values_t):
    rows = q_slots.shape[0]
    span = keys.shape[0]
    homes = rows // PAIR
    vmem = pl.BlockSpec(memory_space=pltpu.VMEM)
    return pl.pallas_call(
        prefix_kernel,
        out_shape=jax.ShapeDtypeStruct((homes * SENT, HD), jnp.int16),
        in_specs=[vmem] * 3,
        out_specs=vmem,
        scratch_shapes=[
            pltpu.VMEM((span, BLOCK), jnp.float32),
            pltpu.VMEM((span, BLOCK), jnp.float32),
            pltpu.VMEM((8, BLOCK), jnp.float32),
            pltpu.VMEM((8, BLOCK), jnp.float32),
        ],
        cost_estimate=pl.CostEstimate(
            flops=4 * rows * span * HD,
            bytes_accessed=keys.size * 4,
            transcendentals=rows * span,
        ),
        compiler_params=pltpu.CompilerParams(vmem_limit_bytes=24 << 20),
        name="prefix_attend",
    )(q_slots, keys, values_t)


def combine_kernel(
    slot_ref, back_ref, part_ref, lse_ref, out_ref, back32_ref, tile_ref
):
    tensor, rows, width = out_ref.shape
    lane = lax.broadcasted_iota(jnp.int32, (GROUP, HD), 1)
    head = lax.broadcasted_iota(jnp.int32, (GROUP, HD), 0)
    own = (slot_ref[tensor * rows] % (HD // PAIR)) * PAIR
    own_step = (own + HD // 2) % HD
    for k in range(0, back_ref.shape[0], 16):
        back32_ref[k : k + 16, :] = back_ref[k : k + 16, :].astype(jnp.int32).astype(jnp.float32)
    for t in range(tensor):
        for i in range(rows):
            r = t * rows + i
            slot = slot_ref[r]
            base = (slot // SLOTS) * SENT
            inner = (slot % SLOTS) * GROUP
            upper = back32_ref[pl.ds(base + PAIR, 1), :]
            lower = back32_ref[pl.ds(base + PAIR + 1, 1), :]
            at = head + inner

            def pick(row, where):
                wide = jnp.broadcast_to(row, (GROUP, HD))
                return jnp.sum(jnp.where(lane == where, wide, 0.0), axis=-1, keepdims=True)

            lse = pick(upper * 0.25 + lower * (1.0 / 131072.0), at + own)
            step = pick(upper, at + own_step)
            scale = jnp.exp2(step * 0.125) * (1.0 / CODE_TOP)
            part = back32_ref[pl.ds(base + inner, GROUP), :] * scale
            suffix_lse = lse_ref[r]
            joint = jnp.maximum(suffix_lse, lse)
            prefix_mass = jnp.exp2(lse - joint)
            suffix_mass = jnp.exp2(suffix_lse - joint)
            result = (prefix_mass * part + suffix_mass * part_ref[r]) / (
                prefix_mass + suffix_mass
            )
            tile_ref[pl.ds(t * GROUP * rows + i, GROUP, stride=rows), :] = result
        for h in range(GROUP):
            out_ref[t, :, h * HD : (h + 1) * HD] = tile_ref[
                pl.ds((t * GROUP + h) * rows, rows), :
            ].astype(jnp.bfloat16)


def combine(slot, back, suffix, tensor):
    count = slot.shape[0] - 1
    vmem = pl.BlockSpec(memory_space=pltpu.VMEM)
    smem = pl.BlockSpec(memory_space=pltpu.SMEM)
    return pl.pallas_call(
        combine_kernel,
        out_shape=jax.ShapeDtypeStruct((tensor, count // tensor, GROUP * HD), jnp.bfloat16),
        in_specs=[smem] + [vmem] * 3,
        out_specs=vmem,
        scratch_shapes=[
            pltpu.VMEM(back.shape, jnp.float32),
            pltpu.VMEM((count * GROUP, HD), jnp.float32),
        ],
        compiler_params=pltpu.CompilerParams(vmem_limit_bytes=8 << 20),
        name="combine",
    )(slot, back, *suffix)


def on_device(queries, suffix_kv, suffix_lengths, prefix_kv, tree_ids, owner_map):
    owners = lax.axis_size("prefix")
    tensor = lax.axis_size("tensor")
    rows = queries.shape[0]
    count = tree_ids.shape[0]
    width = GROUP * HD
    local_q = lax.all_to_all(queries, "tensor", split_axis=1, concat_axis=0, tiled=True)
    q_rows = local_q.reshape(tensor, rows, width)

    prompt = jnp.arange(owner_map.shape[0], dtype=jnp.int32)
    owner_row = jnp.sum(jnp.where(tree_ids[:, None] == prompt[None, :], owner_map[None, :], 0), axis=1)
    place = jnp.arange(count, dtype=jnp.int32)
    earlier = (tree_ids[:, None] == tree_ids[None, :]) & (place[None, :] < place[:, None])
    slot = owner_row * SLOTS + jnp.sum(earlier.astype(jnp.int32), axis=1)

    home = lax.axis_index("prefix").astype(jnp.int32)
    slot = jnp.concatenate([slot, home.reshape(1)])
    outgoing, q_home = dispatch(slot, q_rows)
    arrived = lax.all_to_all(
        outgoing.reshape(owners, SLOTS * GROUP, HD), "prefix", split_axis=0, concat_axis=0, tiled=True
    )
    *suffix, keys, values_t = suffix_attend(suffix_lengths, q_home, suffix_kv[:, :, 0], prefix_kv)
    packed = prefix_attend(arrived.reshape(owners * PAIR, HD), keys, values_t)
    back = lax.all_to_all(
        packed.reshape(owners, SENT // 2, 2, HD), "prefix", split_axis=0, concat_axis=0, tiled=True
    )
    attended = combine(slot, back.reshape(owners * SENT, HD), suffix, tensor)
    done = lax.all_to_all(attended, "tensor", split_axis=0, concat_axis=0, tiled=True)
    return jnp.swapaxes(done, 0, 1).reshape(rows, tensor * width)


def solution(mesh):
    in_specs = (
        P(("prefix", "tensor"), None),
        P("prefix", None, "tensor", None, None),
        P("prefix"),
        P("prefix", None, "tensor", None, None),
        P("prefix"),
        P(),
    )
    out_specs = P(("prefix", "tensor"), None)
    return jax.shard_map(
        on_device, mesh=mesh, in_specs=in_specs, out_specs=out_specs, check_vma=False
    )
```

```python
import math

import jax
import jax.numpy as jnp
from jax import lax
from jax.experimental import pallas as pl
from jax.experimental.pallas import tpu as pltpu
from jax.sharding import PartitionSpec as P

H = 64
KVH = 8
HD = 128
GROUP = H // KVH
SLOTS = 2
CODE_TOP = 32767.0
SCORE_SCALE = math.log2(math.e) / math.sqrt(HD)

BLOCK = 256
CHUNK = 1024
PAIRS = 8
PARTS = 4
PAIR = SLOTS * GROUP
SENT = PAIR + 2

NT = (((1,), (1,)), ((), ()))


def dispatch_kernel(table_ref, q_ref, out_ref, home_ref, tile_ref, stage_ref, sems):
    tensor, rows, width = q_ref.shape
    count = tensor * rows
    for t in range(tensor):
        for h in range(GROUP):
            tile_ref[pl.ds((t * GROUP + h) * rows, rows), :] = q_ref[
                t, :, h * HD : (h + 1) * HD
            ].astype(jnp.float32)
    slots = stage_ref.shape[0]
    size = slots // PARTS
    copies = []
    for part in range(PARTS):
        for s in range(part * size, (part + 1) * size):
            first = table_ref[count + 1 + s]
            tile = tile_ref[pl.ds(first, GROUP, stride=rows), :]
            stage_ref[s] = tile.astype(jnp.bfloat16)
        at = pl.ds(part * size, size)
        copies.append(pltpu.make_async_copy(stage_ref.at[at], out_ref.at[at], sems.at[part]))
        copies[part].start()
    for r in range(0, count, 2):
        pair = []
        for k in range(2):
            t, i = divmod(r + k, rows)
            pair.append(tile_ref[pl.ds(t * GROUP * rows + i, GROUP, stride=rows), :])
        home_ref[r // 2] = jnp.concatenate(pair, axis=0).astype(jnp.bfloat16)
    for part in range(PARTS):
        copies[part].wait()


def dispatch(table, q_rows, slots):
    tensor, rows, width = q_rows.shape
    count = tensor * rows
    vmem = pl.BlockSpec(memory_space=pltpu.VMEM)
    return pl.pallas_call(
        dispatch_kernel,
        out_shape=(
            jax.ShapeDtypeStruct((slots, GROUP, HD), jnp.bfloat16),
            jax.ShapeDtypeStruct((count // 2, 2 * GROUP, HD), jnp.bfloat16),
        ),
        in_specs=[pl.BlockSpec(memory_space=pltpu.SMEM), vmem],
        out_specs=(pl.BlockSpec(memory_space=pltpu.HBM), vmem),
        scratch_shapes=[
            pltpu.VMEM((count * GROUP, HD), jnp.float32),
            pltpu.VMEM((slots, GROUP, HD), jnp.bfloat16),
            pltpu.SemaphoreType.DMA((PARTS,)),
        ],
        compiler_params=pltpu.CompilerParams(vmem_limit_bytes=8 << 20),
        name="dispatch",
    )(table, q_rows)


def suffix_kernel(length_ref, q_ref, kv_ref, prefix_ref, part_ref, lse_ref, keys_ref, turned_ref):
    pairs = q_ref.shape[0]
    span = kv_ref.shape[2]
    lane = lax.broadcasted_iota(jnp.int32, (2 * GROUP, 2 * span), 1)
    second = lax.broadcasted_iota(jnp.int32, (2 * GROUP, 2 * span), 0) >= GROUP
    first_lane = jnp.where(second, span, 0)

    def some_pairs(first):
        scores, live = [], []
        for u in range(PAIRS):
            p = first + u
            keys = kv_ref[pl.ds(2 * p, 2), 0].reshape(2 * span, HD)
            scores.append(
                lax.dot_general(q_ref[p], keys, NT, preferred_element_type=jnp.float32)
            )
            end_lane = first_lane + jnp.where(second, length_ref[2 * p + 1], length_ref[2 * p])
            live.append((lane >= first_lane) & (lane < end_lane))
        masked = [
            jnp.where(m, x * SCORE_SCALE, -jnp.inf) for m, x in zip(live, scores)
        ]
        tops = [jnp.max(x, axis=-1, keepdims=True) for x in masked]
        weights = [jnp.exp2(x - t) for x, t in zip(masked, tops)]
        totals = [jnp.sum(w, axis=-1, keepdims=True) for w in weights]
        sums = []
        for u in range(PAIRS):
            values = kv_ref[pl.ds(2 * (first + u), 2), 1].reshape(2 * span, HD)
            sums.append(
                jnp.dot(
                    weights[u].astype(jnp.bfloat16), values, preferred_element_type=jnp.float32
                )
            )
        shape = (2, GROUP, HD)
        for u in range(PAIRS):
            at = pl.ds(2 * (first + u), 2)
            part_ref[at] = (sums[u] / totals[u]).reshape(shape)
            lse = tops[u] + jnp.log2(totals[u])
            lse_ref[at] = jnp.broadcast_to(lse, (2 * GROUP, HD)).reshape(shape)

    def body(s, carry):
        some_pairs(s * PAIRS)
        return carry

    lax.fori_loop(0, pairs // PAIRS, body, 0)
    keys_ref[...] = prefix_ref[0, 0, 0]
    for k in range(turned_ref.shape[0]):
        turned_ref[k] = prefix_ref[0, 1, 0, k * HD : (k + 1) * HD, :].T


def suffix_attend(lengths, q_home, kv, prefix_kv):
    count = lengths.shape[0]
    span = kv.shape[2]
    out = jax.ShapeDtypeStruct((count, GROUP, HD), jnp.float32)
    vmem = pl.BlockSpec(memory_space=pltpu.VMEM)
    return pl.pallas_call(
        suffix_kernel,
        out_shape=(out, out, jax.ShapeDtypeStruct((prefix_kv.shape[3], HD), jnp.bfloat16), jax.ShapeDtypeStruct((prefix_kv.shape[3] // HD, HD, HD), jnp.bfloat16)),
        in_specs=[pl.BlockSpec(memory_space=pltpu.SMEM), vmem, vmem, vmem],
        out_specs=(vmem, vmem, vmem, vmem),
        cost_estimate=pl.CostEstimate(
            flops=4 * count * GROUP * span * HD,
            bytes_accessed=(kv.size + prefix_kv.size) * 2,
            transcendentals=count * GROUP * span,
        ),
        compiler_params=pltpu.CompilerParams(vmem_limit_bytes=16 << 20),
        name="suffix_attend",
    )(lengths, q_home, kv, prefix_kv)


def prefix_kernel(
    q_ref, k_ref, vt_ref, sent_ref, s0_ref, s1_ref, m0_ref, m1_ref
):
    rows = q_ref.shape[0]
    span = k_ref.shape[0]
    blocks = rows // BLOCK
    chunks = span // CHUNK
    homes = HD // PAIR

    def turned(at):
        tiles = [vt_ref[k] for k in range(at // HD, (at + CHUNK) // HD)]
        return jnp.concatenate(tiles, axis=1)

    def fold(x, op):
        return op(x.reshape(CHUNK // 8, 8, BLOCK), axis=0)

    def finish(now, weighted, mass, shift):
        part = weighted / mass
        largest = jnp.max(jnp.abs(part), axis=0, keepdims=True)
        step = jnp.ceil(jnp.log2(jnp.maximum(largest, 1e-30)) * 8.0)
        code = jnp.round(part * (jnp.exp2(step * -0.125) * CODE_TOP))
        code = jnp.clip(code, -CODE_TOP, CODE_TOP)
        lse = shift + jnp.log2(mass)
        coarse = jnp.round(lse * 4.0)
        fine = jnp.round((lse - coarse * 0.25) * 131072.0)
        lane = lax.broadcasted_iota(jnp.int32, (homes, HD), 1)
        home = lax.broadcasted_iota(jnp.int32, (homes, HD), 0)
        mine = lane // PAIR == home
        other = ((lane + HD // 2) % HD) // PAIR == home
        for g in range(BLOCK // HD):
            cut = slice(g * HD, (g + 1) * HD)
            rows_code = code[:, cut].T
            wide = lambda x: jnp.broadcast_to(x, (homes, HD))
            upper = jnp.where(mine, wide(coarse[:, cut]), 0.0)
            turned = pltpu.roll(wide(step[:, cut]), HD // 2, 1)
            upper = upper + jnp.where(other, turned, 0.0)
            lower = jnp.where(mine, wide(fine[:, cut]), 0.0)
            pieces = []
            for u in range(homes):
                pieces += [
                    rows_code[u * PAIR : (u + 1) * PAIR],
                    upper[u : u + 1],
                    lower[u : u + 1],
                ]
            packed = jnp.concatenate(pieces, axis=0).astype(jnp.int32).astype(jnp.int16)
            size = homes * SENT
            start = pl.multiple_of((now * (BLOCK // HD) + g) * size, size)
            sent_ref[pl.ds(start, size), :] = packed

    def stage(ahead, s_ahead, m_ahead, now, s_now, m_now):
        if ahead is not None:
            q = q_ref[pl.ds(pl.multiple_of(ahead * BLOCK, BLOCK), BLOCK), :]
            top = jnp.full((8, BLOCK), -jnp.inf, jnp.float32)
        if now is not None:
            shift = m_now[0:1, :]
            total = jnp.zeros((8, BLOCK), jnp.float32)
            weighted = [jnp.zeros((HD, BLOCK), jnp.float32)] * 2
        for c in range(chunks):
            at = c * CHUNK
            if ahead is not None:
                scores = lax.dot_general(
                    k_ref[at : at + CHUNK, :], q, NT, preferred_element_type=jnp.float32
                )
                s_ahead[at : at + CHUNK, :] = scores
                top = jnp.maximum(top, fold(scores, jnp.max))
            if now is not None:
                w = jnp.exp2(s_now[at : at + CHUNK, :] * SCORE_SCALE - shift)
                total = total + fold(w, jnp.sum)
                weighted[c % 2] = weighted[c % 2] + jnp.dot(
                    turned(at),
                    w.astype(jnp.bfloat16),
                    preferred_element_type=jnp.float32,
                )
        if ahead is not None:
            m_ahead[...] = jnp.broadcast_to(
                jnp.max(top, axis=0, keepdims=True) * SCORE_SCALE, (8, BLOCK)
            )
        if now is not None:
            finish(now, weighted[0] + weighted[1], jnp.sum(total, axis=0, keepdims=True), shift)

    stage(0, s0_ref, m0_ref, None, None, None)
    for b in range(blocks - 1):
        even, odd = (s0_ref, m0_ref), (s1_ref, m1_ref)
        if b % 2 == 0:
            stage(b + 1, *odd, b, *even)
        else:
            stage(b + 1, *even, b, *odd)
    stage(None, None, None, blocks - 1, s1_ref, m1_ref)


def prefix_attend(q_slots, keys, values_t):
    rows = q_slots.shape[0]
    span = keys.shape[0]
    homes = rows // PAIR
    vmem = pl.BlockSpec(memory_space=pltpu.VMEM)
    return pl.pallas_call(
        prefix_kernel,
        out_shape=jax.ShapeDtypeStruct((homes * SENT, HD), jnp.int16),
        in_specs=[vmem] * 3,
        out_specs=vmem,
        scratch_shapes=[
            pltpu.VMEM((span, BLOCK), jnp.float32),
            pltpu.VMEM((span, BLOCK), jnp.float32),
            pltpu.VMEM((8, BLOCK), jnp.float32),
            pltpu.VMEM((8, BLOCK), jnp.float32),
        ],
        cost_estimate=pl.CostEstimate(
            flops=4 * rows * span * HD,
            bytes_accessed=keys.size * 4,
            transcendentals=rows * span,
        ),
        compiler_params=pltpu.CompilerParams(vmem_limit_bytes=24 << 20),
        name="prefix_attend",
    )(q_slots, keys, values_t)


def combine_kernel(
    table_ref, back_ref, part_ref, lse_ref, out_ref, back32_ref, tile_ref
):
    tensor, rows, width = out_ref.shape
    lane = lax.broadcasted_iota(jnp.int32, (GROUP, HD), 1)
    head = lax.broadcasted_iota(jnp.int32, (GROUP, HD), 0)
    own = (table_ref[tensor * rows] % (HD // PAIR)) * PAIR
    own_step = (own + HD // 2) % HD
    for k in range(0, back_ref.shape[0], 16):
        back32_ref[k : k + 16, :] = back_ref[k : k + 16, :].astype(jnp.int32).astype(jnp.float32)
    for t in range(tensor):
        for i in range(rows):
            r = t * rows + i
            slot = table_ref[r]
            base = (slot // SLOTS) * SENT
            inner = (slot % SLOTS) * GROUP
            upper = back32_ref[pl.ds(base + PAIR, 1), :]
            lower = back32_ref[pl.ds(base + PAIR + 1, 1), :]
            at = head + inner

            def pick(row, where):
                wide = jnp.broadcast_to(row, (GROUP, HD))
                return jnp.sum(jnp.where(lane == where, wide, 0.0), axis=-1, keepdims=True)

            lse = pick(upper * 0.25 + lower * (1.0 / 131072.0), at + own)
            step = pick(upper, at + own_step)
            scale = jnp.exp2(step * 0.125) * (1.0 / CODE_TOP)
            part = back32_ref[pl.ds(base + inner, GROUP), :] * scale
            suffix_lse = lse_ref[r]
            joint = jnp.maximum(suffix_lse, lse)
            prefix_mass = jnp.exp2(lse - joint)
            suffix_mass = jnp.exp2(suffix_lse - joint)
            result = (prefix_mass * part + suffix_mass * part_ref[r]) / (
                prefix_mass + suffix_mass
            )
            tile_ref[pl.ds(t * GROUP * rows + i, GROUP, stride=rows), :] = result
        for h in range(GROUP):
            out_ref[t, :, h * HD : (h + 1) * HD] = tile_ref[
                pl.ds((t * GROUP + h) * rows, rows), :
            ].astype(jnp.bfloat16)


def combine(table, back, suffix, tensor):
    count = suffix[0].shape[0]
    vmem = pl.BlockSpec(memory_space=pltpu.VMEM)
    smem = pl.BlockSpec(memory_space=pltpu.SMEM)
    return pl.pallas_call(
        combine_kernel,
        out_shape=jax.ShapeDtypeStruct((tensor, count // tensor, GROUP * HD), jnp.bfloat16),
        in_specs=[smem] + [vmem] * 3,
        out_specs=vmem,
        scratch_shapes=[
            pltpu.VMEM(back.shape, jnp.float32),
            pltpu.VMEM((count * GROUP, HD), jnp.float32),
        ],
        compiler_params=pltpu.CompilerParams(vmem_limit_bytes=8 << 20),
        name="combine",
    )(table, back, *suffix)


def on_device(queries, suffix_kv, suffix_lengths, prefix_kv, tree_ids, owner_map):
    owners = lax.axis_size("prefix")
    tensor = lax.axis_size("tensor")
    rows = queries.shape[0]
    count = tree_ids.shape[0]
    width = GROUP * HD
    local_q = lax.all_to_all(queries, "tensor", split_axis=1, concat_axis=0, tiled=True)
    q_rows = local_q.reshape(tensor, rows, width)

    prompt = jnp.arange(owner_map.shape[0], dtype=jnp.int32)
    owner_row = jnp.sum(jnp.where(tree_ids[:, None] == prompt[None, :], owner_map[None, :], 0), axis=1)
    place = jnp.arange(count, dtype=jnp.int32)
    earlier = (tree_ids[:, None] == tree_ids[None, :]) & (place[None, :] < place[:, None])
    slot = owner_row * SLOTS + jnp.sum(earlier.astype(jnp.int32), axis=1)

    home = lax.axis_index("prefix").astype(jnp.int32)
    first = (place // rows) * (GROUP * rows) + place % rows
    slots = jnp.arange(owners * SLOTS, dtype=jnp.int32)
    pick = jnp.sum(jnp.where(slots[:, None] == slot[None, :], first[None, :], 0), axis=1)
    table = jnp.concatenate([slot, home.reshape(1), pick])
    outgoing, q_home = dispatch(table, q_rows, owners * SLOTS)
    arrived = lax.all_to_all(
        outgoing.reshape(owners, SLOTS * GROUP, HD), "prefix", split_axis=0, concat_axis=0, tiled=True
    )
    *suffix, keys, values_t = suffix_attend(suffix_lengths, q_home, suffix_kv[:, :, 0], prefix_kv)
    packed = prefix_attend(arrived.reshape(owners * PAIR, HD), keys, values_t)
    back = lax.all_to_all(
        packed.reshape(owners, SENT // 2, 2, HD), "prefix", split_axis=0, concat_axis=0, tiled=True
    )
    attended = combine(table, back.reshape(owners * SENT, HD), suffix, tensor)
    done = lax.all_to_all(attended, "tensor", split_axis=0, concat_axis=0, tiled=True)
    return jnp.swapaxes(done, 0, 1).reshape(rows, tensor * width)


def solution(mesh):
    in_specs = (
        P(("prefix", "tensor"), None),
        P("prefix", None, "tensor", None, None),
        P("prefix"),
        P("prefix", None, "tensor", None, None),
        P("prefix"),
        P(),
    )
    out_specs = P(("prefix", "tensor"), None)
    return jax.shard_map(
        on_device, mesh=mesh, in_specs=in_specs, out_specs=out_specs, check_vma=False
    )
```

```python
import math

import jax
import jax.numpy as jnp
from jax import lax
from jax.experimental import pallas as pl
from jax.experimental.pallas import tpu as pltpu
from jax.sharding import PartitionSpec as P

H = 64
KVH = 8
HD = 128
GROUP = H // KVH
SLOTS = 2
CODE_TOP = 32767.0
SCORE_SCALE = math.log2(math.e) / math.sqrt(HD)

BLOCK = 256
CHUNK = 1024
PAIRS = 8
PARTS = 4
PAIR = SLOTS * GROUP
SENT = PAIR + 2

NT = (((1,), (1,)), ((), ()))


def dispatch_kernel(
    table_in_ref, q_ref, out_ref, home_ref, tile_ref, stage_ref, sems, table_ref, table_sem
):
    table_copy = pltpu.make_async_copy(table_in_ref, table_ref, table_sem)
    table_copy.start()
    tensor, rows, width = q_ref.shape
    count = tensor * rows
    for t in range(tensor):
        for h in range(GROUP):
            tile_ref[pl.ds((t * GROUP + h) * rows, rows), :] = q_ref[
                t, :, h * HD : (h + 1) * HD
            ].astype(jnp.float32)
    table_copy.wait()
    slots = stage_ref.shape[0]
    size = slots // PARTS
    copies = []
    for part in range(PARTS):
        for s in range(part * size, (part + 1) * size):
            first = table_ref[count + 1 + s]
            tile = tile_ref[pl.ds(first, GROUP, stride=rows), :]
            stage_ref[s] = tile.astype(jnp.bfloat16)
        at = pl.ds(part * size, size)
        copies.append(pltpu.make_async_copy(stage_ref.at[at], out_ref.at[at], sems.at[part]))
        copies[part].start()
    for r in range(0, count, 2):
        pair = []
        for k in range(2):
            t, i = divmod(r + k, rows)
            pair.append(tile_ref[pl.ds(t * GROUP * rows + i, GROUP, stride=rows), :])
        home_ref[r // 2] = jnp.concatenate(pair, axis=0).astype(jnp.bfloat16)
    for part in range(PARTS):
        copies[part].wait()


def dispatch(table, q_rows, slots):
    tensor, rows, width = q_rows.shape
    count = tensor * rows
    vmem = pl.BlockSpec(memory_space=pltpu.VMEM)
    return pl.pallas_call(
        dispatch_kernel,
        out_shape=(
            jax.ShapeDtypeStruct((slots, GROUP, HD), jnp.bfloat16),
            jax.ShapeDtypeStruct((count // 2, 2 * GROUP, HD), jnp.bfloat16),
        ),
        in_specs=[pl.BlockSpec(memory_space=pl.ANY), vmem],
        out_specs=(pl.BlockSpec(memory_space=pltpu.HBM), vmem),
        scratch_shapes=[
            pltpu.VMEM((count * GROUP, HD), jnp.float32),
            pltpu.VMEM((slots, GROUP, HD), jnp.bfloat16),
            pltpu.SemaphoreType.DMA((PARTS,)),
            pltpu.SMEM(table.shape, jnp.int32),
            pltpu.SemaphoreType.DMA,
        ],
        compiler_params=pltpu.CompilerParams(vmem_limit_bytes=8 << 20),
        name="dispatch",
    )(table, q_rows)


def suffix_kernel(length_ref, q_ref, kv_ref, prefix_ref, part_ref, lse_ref, keys_ref, turned_ref):
    pairs = q_ref.shape[0]
    span = kv_ref.shape[2]
    lane = lax.broadcasted_iota(jnp.int32, (2 * GROUP, 2 * span), 1)
    second = lax.broadcasted_iota(jnp.int32, (2 * GROUP, 2 * span), 0) >= GROUP
    first_lane = jnp.where(second, span, 0)

    def some_pairs(first):
        scores, live = [], []
        for u in range(PAIRS):
            p = first + u
            keys = kv_ref[pl.ds(2 * p, 2), 0].reshape(2 * span, HD)
            scores.append(
                lax.dot_general(q_ref[p], keys, NT, preferred_element_type=jnp.float32)
            )
            end_lane = first_lane + jnp.where(second, length_ref[2 * p + 1], length_ref[2 * p])
            live.append((lane >= first_lane) & (lane < end_lane))
        masked = [
            jnp.where(m, x * SCORE_SCALE, -jnp.inf) for m, x in zip(live, scores)
        ]
        tops = [jnp.max(x, axis=-1, keepdims=True) for x in masked]
        weights = [jnp.exp2(x - t) for x, t in zip(masked, tops)]
        totals = [jnp.sum(w, axis=-1, keepdims=True) for w in weights]
        sums = []
        for u in range(PAIRS):
            values = kv_ref[pl.ds(2 * (first + u), 2), 1].reshape(2 * span, HD)
            sums.append(
                jnp.dot(
                    weights[u].astype(jnp.bfloat16), values, preferred_element_type=jnp.float32
                )
            )
        shape = (2, GROUP, HD)
        for u in range(PAIRS):
            at = pl.ds(2 * (first + u), 2)
            part_ref[at] = (sums[u] / totals[u]).reshape(shape)
            lse = tops[u] + jnp.log2(totals[u])
            lse_ref[at] = jnp.broadcast_to(lse, (2 * GROUP, HD)).reshape(shape)

    def body(s, carry):
        some_pairs(s * PAIRS)
        return carry

    lax.fori_loop(0, pairs // PAIRS, body, 0)
    keys_ref[...] = prefix_ref[0, 0, 0]
    for k in range(turned_ref.shape[0]):
        turned_ref[k] = prefix_ref[0, 1, 0, k * HD : (k + 1) * HD, :].T


def suffix_attend(lengths, q_home, kv, prefix_kv):
    count = lengths.shape[0]
    span = kv.shape[2]
    out = jax.ShapeDtypeStruct((count, GROUP, HD), jnp.float32)
    vmem = pl.BlockSpec(memory_space=pltpu.VMEM)
    return pl.pallas_call(
        suffix_kernel,
        out_shape=(out, out, jax.ShapeDtypeStruct((prefix_kv.shape[3], HD), jnp.bfloat16), jax.ShapeDtypeStruct((prefix_kv.shape[3] // HD, HD, HD), jnp.bfloat16)),
        in_specs=[pl.BlockSpec(memory_space=pltpu.SMEM), vmem, vmem, vmem],
        out_specs=(vmem, vmem, vmem, vmem),
        cost_estimate=pl.CostEstimate(
            flops=4 * count * GROUP * span * HD,
            bytes_accessed=(kv.size + prefix_kv.size) * 2,
            transcendentals=count * GROUP * span,
        ),
        compiler_params=pltpu.CompilerParams(vmem_limit_bytes=16 << 20),
        name="suffix_attend",
    )(lengths, q_home, kv, prefix_kv)


def prefix_kernel(
    q_ref, k_ref, vt_ref, sent_ref, s0_ref, s1_ref, m0_ref, m1_ref
):
    rows = q_ref.shape[0]
    span = k_ref.shape[0]
    blocks = rows // BLOCK
    chunks = span // CHUNK
    homes = HD // PAIR

    def turned(at):
        tiles = [vt_ref[k] for k in range(at // HD, (at + CHUNK) // HD)]
        return jnp.concatenate(tiles, axis=1)

    def fold(x, op):
        return op(x.reshape(CHUNK // 8, 8, BLOCK), axis=0)

    def finish(now, weighted, mass, shift):
        part = weighted / mass
        largest = jnp.max(jnp.abs(part), axis=0, keepdims=True)
        step = jnp.ceil(jnp.log2(jnp.maximum(largest, 1e-30)) * 8.0)
        code = jnp.round(part * (jnp.exp2(step * -0.125) * CODE_TOP))
        code = jnp.clip(code, -CODE_TOP, CODE_TOP)
        lse = shift + jnp.log2(mass)
        coarse = jnp.round(lse * 4.0)
        fine = jnp.round((lse - coarse * 0.25) * 131072.0)
        lane = lax.broadcasted_iota(jnp.int32, (homes, HD), 1)
        home = lax.broadcasted_iota(jnp.int32, (homes, HD), 0)
        mine = lane // PAIR == home
        other = ((lane + HD // 2) % HD) // PAIR == home
        for g in range(BLOCK // HD):
            cut = slice(g * HD, (g + 1) * HD)
            rows_code = code[:, cut].T
            wide = lambda x: jnp.broadcast_to(x, (homes, HD))
            upper = jnp.where(mine, wide(coarse[:, cut]), 0.0)
            turned = pltpu.roll(wide(step[:, cut]), HD // 2, 1)
            upper = upper + jnp.where(other, turned, 0.0)
            lower = jnp.where(mine, wide(fine[:, cut]), 0.0)
            pieces = []
            for u in range(homes):
                pieces += [
                    rows_code[u * PAIR : (u + 1) * PAIR],
                    upper[u : u + 1],
                    lower[u : u + 1],
                ]
            packed = jnp.concatenate(pieces, axis=0).astype(jnp.int32).astype(jnp.int16)
            size = homes * SENT
            start = pl.multiple_of((now * (BLOCK // HD) + g) * size, size)
            sent_ref[pl.ds(start, size), :] = packed

    def stage(ahead, s_ahead, m_ahead, now, s_now, m_now):
        if ahead is not None:
            q = q_ref[pl.ds(pl.multiple_of(ahead * BLOCK, BLOCK), BLOCK), :]
            top = jnp.full((8, BLOCK), -jnp.inf, jnp.float32)
        if now is not None:
            shift = m_now[0:1, :]
            total = jnp.zeros((8, BLOCK), jnp.float32)
            weighted = [jnp.zeros((HD, BLOCK), jnp.float32)] * 2
        for c in range(chunks):
            at = c * CHUNK
            if ahead is not None:
                scores = lax.dot_general(
                    k_ref[at : at + CHUNK, :], q, NT, preferred_element_type=jnp.float32
                )
                s_ahead[at : at + CHUNK, :] = scores
                top = jnp.maximum(top, fold(scores, jnp.max))
            if now is not None:
                w = jnp.exp2(s_now[at : at + CHUNK, :] * SCORE_SCALE - shift)
                total = total + fold(w, jnp.sum)
                weighted[c % 2] = weighted[c % 2] + jnp.dot(
                    turned(at),
                    w.astype(jnp.bfloat16),
                    preferred_element_type=jnp.float32,
                )
        if ahead is not None:
            m_ahead[...] = jnp.broadcast_to(
                jnp.max(top, axis=0, keepdims=True) * SCORE_SCALE, (8, BLOCK)
            )
        if now is not None:
            finish(now, weighted[0] + weighted[1], jnp.sum(total, axis=0, keepdims=True), shift)

    stage(0, s0_ref, m0_ref, None, None, None)
    for b in range(blocks - 1):
        even, odd = (s0_ref, m0_ref), (s1_ref, m1_ref)
        if b % 2 == 0:
            stage(b + 1, *odd, b, *even)
        else:
            stage(b + 1, *even, b, *odd)
    stage(None, None, None, blocks - 1, s1_ref, m1_ref)


def prefix_attend(q_slots, keys, values_t):
    rows = q_slots.shape[0]
    span = keys.shape[0]
    homes = rows // PAIR
    vmem = pl.BlockSpec(memory_space=pltpu.VMEM)
    return pl.pallas_call(
        prefix_kernel,
        out_shape=jax.ShapeDtypeStruct((homes * SENT, HD), jnp.int16),
        in_specs=[vmem] * 3,
        out_specs=vmem,
        scratch_shapes=[
            pltpu.VMEM((span, BLOCK), jnp.float32),
            pltpu.VMEM((span, BLOCK), jnp.float32),
            pltpu.VMEM((8, BLOCK), jnp.float32),
            pltpu.VMEM((8, BLOCK), jnp.float32),
        ],
        cost_estimate=pl.CostEstimate(
            flops=4 * rows * span * HD,
            bytes_accessed=keys.size * 4,
            transcendentals=rows * span,
        ),
        compiler_params=pltpu.CompilerParams(vmem_limit_bytes=24 << 20),
        name="prefix_attend",
    )(q_slots, keys, values_t)


def combine_kernel(
    table_in_ref, back_ref, part_ref, lse_ref, out_ref, back32_ref, tile_ref, table_ref, table_sem
):
    table_copy = pltpu.make_async_copy(table_in_ref, table_ref, table_sem)
    table_copy.start()
    tensor, rows, width = out_ref.shape
    lane = lax.broadcasted_iota(jnp.int32, (GROUP, HD), 1)
    head = lax.broadcasted_iota(jnp.int32, (GROUP, HD), 0)
    for k in range(0, back_ref.shape[0], 16):
        back32_ref[k : k + 16, :] = back_ref[k : k + 16, :].astype(jnp.int32).astype(jnp.float32)
    table_copy.wait()
    own = (table_ref[tensor * rows] % (HD // PAIR)) * PAIR
    own_step = (own + HD // 2) % HD
    for t in range(tensor):
        for i in range(rows):
            r = t * rows + i
            slot = table_ref[r]
            base = (slot // SLOTS) * SENT
            inner = (slot % SLOTS) * GROUP
            upper = back32_ref[pl.ds(base + PAIR, 1), :]
            lower = back32_ref[pl.ds(base + PAIR + 1, 1), :]
            at = head + inner

            def pick(row, where):
                wide = jnp.broadcast_to(row, (GROUP, HD))
                return jnp.sum(jnp.where(lane == where, wide, 0.0), axis=-1, keepdims=True)

            lse = pick(upper * 0.25 + lower * (1.0 / 131072.0), at + own)
            step = pick(upper, at + own_step)
            scale = jnp.exp2(step * 0.125) * (1.0 / CODE_TOP)
            part = back32_ref[pl.ds(base + inner, GROUP), :] * scale
            suffix_lse = lse_ref[r]
            joint = jnp.maximum(suffix_lse, lse)
            prefix_mass = jnp.exp2(lse - joint)
            suffix_mass = jnp.exp2(suffix_lse - joint)
            result = (prefix_mass * part + suffix_mass * part_ref[r]) / (
                prefix_mass + suffix_mass
            )
            tile_ref[pl.ds(t * GROUP * rows + i, GROUP, stride=rows), :] = result
        for h in range(GROUP):
            out_ref[t, :, h * HD : (h + 1) * HD] = tile_ref[
                pl.ds((t * GROUP + h) * rows, rows), :
            ].astype(jnp.bfloat16)


def combine(table, back, suffix, tensor):
    count = suffix[0].shape[0]
    vmem = pl.BlockSpec(memory_space=pltpu.VMEM)
    return pl.pallas_call(
        combine_kernel,
        out_shape=jax.ShapeDtypeStruct((tensor, count // tensor, GROUP * HD), jnp.bfloat16),
        in_specs=[pl.BlockSpec(memory_space=pl.ANY)] + [vmem] * 3,
        out_specs=vmem,
        scratch_shapes=[
            pltpu.VMEM(back.shape, jnp.float32),
            pltpu.VMEM((count * GROUP, HD), jnp.float32),
            pltpu.SMEM(table.shape, jnp.int32),
            pltpu.SemaphoreType.DMA,
        ],
        compiler_params=pltpu.CompilerParams(vmem_limit_bytes=8 << 20),
        name="combine",
    )(table, back, *suffix)


def on_device(queries, suffix_kv, suffix_lengths, prefix_kv, tree_ids, owner_map):
    owners = lax.axis_size("prefix")
    tensor = lax.axis_size("tensor")
    rows = queries.shape[0]
    count = tree_ids.shape[0]
    width = GROUP * HD
    local_q = lax.all_to_all(queries, "tensor", split_axis=1, concat_axis=0, tiled=True)
    q_rows = local_q.reshape(tensor, rows, width)

    prompt = jnp.arange(owner_map.shape[0], dtype=jnp.int32)
    owner_row = jnp.sum(jnp.where(tree_ids[:, None] == prompt[None, :], owner_map[None, :], 0), axis=1)
    place = jnp.arange(count, dtype=jnp.int32)
    earlier = (tree_ids[:, None] == tree_ids[None, :]) & (place[None, :] < place[:, None])
    slot = owner_row * SLOTS + jnp.sum(earlier.astype(jnp.int32), axis=1)

    home = lax.axis_index("prefix").astype(jnp.int32)
    first = (place // rows) * (GROUP * rows) + place % rows
    slots = jnp.arange(owners * SLOTS, dtype=jnp.int32)
    pick = jnp.sum(jnp.where(slots[:, None] == slot[None, :], first[None, :], 0), axis=1)
    table = jnp.concatenate([slot, home.reshape(1), pick])
    table = jnp.pad(table, (0, -table.shape[0] % (2 * HD)))
    outgoing, q_home = dispatch(table, q_rows, owners * SLOTS)
    arrived = lax.all_to_all(
        outgoing.reshape(owners, SLOTS * GROUP, HD), "prefix", split_axis=0, concat_axis=0, tiled=True
    )
    *suffix, keys, values_t = suffix_attend(suffix_lengths, q_home, suffix_kv[:, :, 0], prefix_kv)
    packed = prefix_attend(arrived.reshape(owners * PAIR, HD), keys, values_t)
    back = lax.all_to_all(
        packed.reshape(owners, SENT // 2, 2, HD), "prefix", split_axis=0, concat_axis=0, tiled=True
    )
    attended = combine(table, back.reshape(owners * SENT, HD), suffix, tensor)
    done = lax.all_to_all(attended, "tensor", split_axis=0, concat_axis=0, tiled=True)
    return jnp.swapaxes(done, 0, 1).reshape(rows, tensor * width)


def solution(mesh):
    in_specs = (
        P(("prefix", "tensor"), None),
        P("prefix", None, "tensor", None, None),
        P("prefix"),
        P("prefix", None, "tensor", None, None),
        P("prefix"),
        P(),
    )
    out_specs = P(("prefix", "tensor"), None)
    return jax.shard_map(
        on_device, mesh=mesh, in_specs=in_specs, out_specs=out_specs, check_vma=False
    )
```

```python
import math

import jax
import jax.numpy as jnp
from jax import lax
from jax.experimental import pallas as pl
from jax.experimental.pallas import tpu as pltpu
from jax.sharding import PartitionSpec as P

H = 64
KVH = 8
HD = 128
GROUP = H // KVH
SLOTS = 2
CODE_TOP = 32767.0
SCORE_SCALE = math.log2(math.e) / math.sqrt(HD)

BLOCK = 256
CHUNK = 1024
PAIRS = 8
PAIR = SLOTS * GROUP
SENT = PAIR + 2

NT = (((1,), (1,)), ((), ()))


def dispatch_kernel(slot_ref, q_ref, out_ref, home_ref, tile_ref):
    tensor, rows, width = q_ref.shape
    out_ref[...] = jnp.zeros_like(out_ref)
    for t in range(tensor):
        for h in range(GROUP):
            tile_ref[pl.ds((t * GROUP + h) * rows, rows), :] = q_ref[
                t, :, h * HD : (h + 1) * HD
            ].astype(jnp.float32)
    for r in range(0, tensor * rows, 2):
        pair = []
        for k in range(2):
            t, i = divmod(r + k, rows)
            tile = tile_ref[pl.ds(t * GROUP * rows + i, GROUP, stride=rows), :]
            pair.append(tile)
            out_ref[slot_ref[r + k]] = tile.astype(jnp.bfloat16)
        home_ref[r // 2] = jnp.concatenate(pair, axis=0).astype(jnp.bfloat16)


def dispatch(slot, q_rows):
    tensor, rows, width = q_rows.shape
    count = tensor * rows
    owners = count
    return pl.pallas_call(
        dispatch_kernel,
        out_shape=(
            jax.ShapeDtypeStruct((owners * SLOTS, GROUP, HD), jnp.bfloat16),
            jax.ShapeDtypeStruct((count // 2, 2 * GROUP, HD), jnp.bfloat16),
        ),
        in_specs=[
            pl.BlockSpec(memory_space=pltpu.SMEM),
            pl.BlockSpec(memory_space=pltpu.VMEM),
        ],
        out_specs=(
            pl.BlockSpec(memory_space=pltpu.VMEM),
            pl.BlockSpec(memory_space=pltpu.VMEM),
        ),
        scratch_shapes=[pltpu.VMEM((count * GROUP, HD), jnp.float32)],
        compiler_params=pltpu.CompilerParams(vmem_limit_bytes=8 << 20),
        name="dispatch",
    )(slot, q_rows)


def suffix_kernel(length_ref, q_ref, kv_ref, prefix_ref, part_ref, lse_ref, keys_ref, turned_ref):
    pairs = q_ref.shape[0]
    span = kv_ref.shape[2]
    lane = lax.broadcasted_iota(jnp.int32, (2 * GROUP, 2 * span), 1)
    second = lax.broadcasted_iota(jnp.int32, (2 * GROUP, 2 * span), 0) >= GROUP
    first_lane = jnp.where(second, span, 0)

    def some_pairs(first):
        scores, live = [], []
        for u in range(PAIRS):
            p = first + u
            keys = kv_ref[pl.ds(2 * p, 2), 0].reshape(2 * span, HD)
            scores.append(
                lax.dot_general(q_ref[p], keys, NT, preferred_element_type=jnp.float32)
            )
            end_lane = first_lane + jnp.where(second, length_ref[2 * p + 1], length_ref[2 * p])
            live.append((lane >= first_lane) & (lane < end_lane))
        masked = [
            jnp.where(m, x * SCORE_SCALE, -jnp.inf) for m, x in zip(live, scores)
        ]
        tops = [jnp.max(x, axis=-1, keepdims=True) for x in masked]
        weights = [jnp.exp2(x - t) for x, t in zip(masked, tops)]
        totals = [jnp.sum(w, axis=-1, keepdims=True) for w in weights]
        sums = []
        for u in range(PAIRS):
            values = kv_ref[pl.ds(2 * (first + u), 2), 1].reshape(2 * span, HD)
            sums.append(
                jnp.dot(
                    weights[u].astype(jnp.bfloat16), values, preferred_element_type=jnp.float32
                )
            )
        shape = (2, GROUP, HD)
        for u in range(PAIRS):
            at = pl.ds(2 * (first + u), 2)
            part_ref[at] = (sums[u] / totals[u]).reshape(shape)
            lse = tops[u] + jnp.log2(totals[u])
            lse_ref[at] = jnp.broadcast_to(lse, (2 * GROUP, HD)).reshape(shape)

    def body(s, carry):
        some_pairs(s * PAIRS)
        return carry

    lax.fori_loop(0, pairs // PAIRS, body, 0)
    keys_ref[...] = prefix_ref[0, 0, 0]
    for k in range(turned_ref.shape[0]):
        turned_ref[k] = prefix_ref[0, 1, 0, k * HD : (k + 1) * HD, :].T


def suffix_attend(lengths, q_home, kv, prefix_kv):
    count = lengths.shape[0]
    span = kv.shape[2]
    out = jax.ShapeDtypeStruct((count, GROUP, HD), jnp.float32)
    vmem = pl.BlockSpec(memory_space=pltpu.VMEM)
    return pl.pallas_call(
        suffix_kernel,
        out_shape=(out, out, jax.ShapeDtypeStruct((prefix_kv.shape[3], HD), jnp.bfloat16), jax.ShapeDtypeStruct((prefix_kv.shape[3] // HD, HD, HD), jnp.bfloat16)),
        in_specs=[pl.BlockSpec(memory_space=pltpu.SMEM), vmem, vmem, vmem],
        out_specs=(vmem, vmem, vmem, vmem),
        cost_estimate=pl.CostEstimate(
            flops=4 * count * GROUP * span * HD,
            bytes_accessed=(kv.size + prefix_kv.size) * 2,
            transcendentals=count * GROUP * span,
        ),
        compiler_params=pltpu.CompilerParams(vmem_limit_bytes=16 << 20),
        name="suffix_attend",
    )(lengths, q_home, kv, prefix_kv)


def prefix_kernel(
    q_ref, k_ref, vt_ref, sent_ref, s0_ref, s1_ref, m0_ref, m1_ref
):
    rows = q_ref.shape[0]
    span = k_ref.shape[0]
    blocks = rows // BLOCK
    chunks = span // CHUNK
    homes = HD // PAIR

    def turned(at):
        tiles = [vt_ref[k] for k in range(at // HD, (at + CHUNK) // HD)]
        return jnp.concatenate(tiles, axis=1)

    def fold(x, op):
        return op(x.reshape(CHUNK // 8, 8, BLOCK), axis=0)

    def finish(now, weighted, mass, shift):
        part = weighted / mass
        largest = jnp.max(jnp.abs(part), axis=0, keepdims=True)
        step = jnp.ceil(jnp.log2(jnp.maximum(largest, 1e-30)) * 8.0)
        code = jnp.round(part * (jnp.exp2(step * -0.125) * CODE_TOP))
        code = jnp.clip(code, -CODE_TOP, CODE_TOP)
        lse = shift + jnp.log2(mass)
        coarse = jnp.round(lse * 4.0)
        fine = jnp.round((lse - coarse * 0.25) * 131072.0)
        lane = lax.broadcasted_iota(jnp.int32, (homes, HD), 1)
        home = lax.broadcasted_iota(jnp.int32, (homes, HD), 0)
        mine = lane // PAIR == home
        other = ((lane + HD // 2) % HD) // PAIR == home
        for g in range(BLOCK // HD):
            cut = slice(g * HD, (g + 1) * HD)
            rows_code = code[:, cut].T
            wide = lambda x: jnp.broadcast_to(x, (homes, HD))
            upper = jnp.where(mine, wide(coarse[:, cut]), 0.0)
            turned = pltpu.roll(wide(step[:, cut]), HD // 2, 1)
            upper = upper + jnp.where(other, turned, 0.0)
            lower = jnp.where(mine, wide(fine[:, cut]), 0.0)
            pieces = []
            for u in range(homes):
                pieces += [
                    rows_code[u * PAIR : (u + 1) * PAIR],
                    upper[u : u + 1],
                    lower[u : u + 1],
                ]
            packed = jnp.concatenate(pieces, axis=0).astype(jnp.int32).astype(jnp.int16)
            size = homes * SENT
            start = pl.multiple_of((now * (BLOCK // HD) + g) * size, size)
            sent_ref[pl.ds(start, size), :] = packed

    def stage(ahead, s_ahead, m_ahead, now, s_now, m_now):
        if ahead is not None:
            q = q_ref[pl.ds(pl.multiple_of(ahead * BLOCK, BLOCK), BLOCK), :]
            top = jnp.full((8, BLOCK), -jnp.inf, jnp.float32)
        if now is not None:
            shift = m_now[0:1, :]
            total = jnp.zeros((8, BLOCK), jnp.float32)
            weighted = [jnp.zeros((HD, BLOCK), jnp.float32)] * 2
        for c in range(chunks):
            at = c * CHUNK
            if ahead is not None:
                scores = lax.dot_general(
                    k_ref[at : at + CHUNK, :], q, NT, preferred_element_type=jnp.float32
                )
                s_ahead[at : at + CHUNK, :] = scores
                top = jnp.maximum(top, fold(scores, jnp.max))
            if now is not None:
                w = jnp.exp2(s_now[at : at + CHUNK, :] * SCORE_SCALE - shift)
                total = total + fold(w, jnp.sum)
                weighted[c % 2] = weighted[c % 2] + jnp.dot(
                    turned(at),
                    w.astype(jnp.bfloat16),
                    preferred_element_type=jnp.float32,
                )
        if ahead is not None:
            m_ahead[...] = jnp.broadcast_to(
                jnp.max(top, axis=0, keepdims=True) * SCORE_SCALE, (8, BLOCK)
            )
        if now is not None:
            finish(now, weighted[0] + weighted[1], jnp.sum(total, axis=0, keepdims=True), shift)

    stage(0, s0_ref, m0_ref, None, None, None)
    for b in range(blocks - 1):
        even, odd = (s0_ref, m0_ref), (s1_ref, m1_ref)
        if b % 2 == 0:
            stage(b + 1, *odd, b, *even)
        else:
            stage(b + 1, *even, b, *odd)
    stage(None, None, None, blocks - 1, s1_ref, m1_ref)


def prefix_attend(q_slots, keys, values_t):
    rows = q_slots.shape[0]
    span = keys.shape[0]
    homes = rows // PAIR
    vmem = pl.BlockSpec(memory_space=pltpu.VMEM)
    return pl.pallas_call(
        prefix_kernel,
        out_shape=jax.ShapeDtypeStruct((homes * SENT, HD), jnp.int16),
        in_specs=[vmem] * 3,
        out_specs=vmem,
        scratch_shapes=[
            pltpu.VMEM((span, BLOCK), jnp.float32),
            pltpu.VMEM((span, BLOCK), jnp.float32),
            pltpu.VMEM((8, BLOCK), jnp.float32),
            pltpu.VMEM((8, BLOCK), jnp.float32),
        ],
        cost_estimate=pl.CostEstimate(
            flops=4 * rows * span * HD,
            bytes_accessed=keys.size * 4,
            transcendentals=rows * span,
        ),
        compiler_params=pltpu.CompilerParams(vmem_limit_bytes=24 << 20),
        name="prefix_attend",
    )(q_slots, keys, values_t)


def combine_kernel(
    slot_ref, back_ref, part_ref, lse_ref, out_ref, back32_ref, tile_ref
):
    tensor, rows, width = out_ref.shape
    lane = lax.broadcasted_iota(jnp.int32, (GROUP, HD), 1)
    head = lax.broadcasted_iota(jnp.int32, (GROUP, HD), 0)
    own = (slot_ref[tensor * rows] % (HD // PAIR)) * PAIR
    own_step = (own + HD // 2) % HD
    for k in range(0, back_ref.shape[0], 16):
        back32_ref[k : k + 16, :] = back_ref[k : k + 16, :].astype(jnp.int32).astype(jnp.float32)
    for t in range(tensor):
        for i in range(rows):
            r = t * rows + i
            slot = slot_ref[r]
            base = (slot // SLOTS) * SENT
            inner = (slot % SLOTS) * GROUP
            upper = back32_ref[pl.ds(base + PAIR, 1), :]
            lower = back32_ref[pl.ds(base + PAIR + 1, 1), :]
            at = head + inner

            def pick(row, where):
                wide = jnp.broadcast_to(row, (GROUP, HD))
                return jnp.sum(jnp.where(lane == where, wide, 0.0), axis=-1, keepdims=True)

            lse = pick(upper * 0.25 + lower * (1.0 / 131072.0), at + own)
            step = pick(upper, at + own_step)
            scale = jnp.exp2(step * 0.125) * (1.0 / CODE_TOP)
            part = back32_ref[pl.ds(base + inner, GROUP), :] * scale
            suffix_lse = lse_ref[r]
            joint = jnp.maximum(suffix_lse, lse)
            prefix_mass = jnp.exp2(lse - joint)
            suffix_mass = jnp.exp2(suffix_lse - joint)
            result = (prefix_mass * part + suffix_mass * part_ref[r]) / (
                prefix_mass + suffix_mass
            )
            tile_ref[pl.ds(t * GROUP * rows + i, GROUP, stride=rows), :] = result
        for h in range(GROUP):
            out_ref[t, :, h * HD : (h + 1) * HD] = tile_ref[
                pl.ds((t * GROUP + h) * rows, rows), :
            ].astype(jnp.bfloat16)


def combine(slot, back, suffix, tensor):
    count = slot.shape[0] - 1
    vmem = pl.BlockSpec(memory_space=pltpu.VMEM)
    smem = pl.BlockSpec(memory_space=pltpu.SMEM)
    return pl.pallas_call(
        combine_kernel,
        out_shape=jax.ShapeDtypeStruct((tensor, count // tensor, GROUP * HD), jnp.bfloat16),
        in_specs=[smem] + [vmem] * 3,
        out_specs=vmem,
        scratch_shapes=[
            pltpu.VMEM(back.shape, jnp.float32),
            pltpu.VMEM((count * GROUP, HD), jnp.float32),
        ],
        compiler_params=pltpu.CompilerParams(vmem_limit_bytes=8 << 20),
        name="combine",
    )(slot, back, *suffix)


def on_device(queries, suffix_kv, suffix_lengths, prefix_kv, tree_ids, owner_map):
    owners = lax.axis_size("prefix")
    tensor = lax.axis_size("tensor")
    rows = queries.shape[0]
    count = tree_ids.shape[0]
    width = GROUP * HD
    local_q = lax.all_to_all(queries, "tensor", split_axis=1, concat_axis=0, tiled=True)
    q_rows = local_q.reshape(tensor, rows, width)

    prompt = jnp.arange(owner_map.shape[0], dtype=jnp.int32)
    owner_row = jnp.sum(jnp.where(tree_ids[:, None] == prompt[None, :], owner_map[None, :], 0), axis=1)
    place = jnp.arange(count, dtype=jnp.int32)
    earlier = (tree_ids[:, None] == tree_ids[None, :]) & (place[None, :] < place[:, None])
    slot = owner_row * SLOTS + jnp.sum(earlier.astype(jnp.int32), axis=1)

    home = lax.axis_index("prefix").astype(jnp.int32)
    slot = jnp.concatenate([slot, home.reshape(1)])
    outgoing, q_home = dispatch(slot, q_rows)
    arrived = lax.all_to_all(
        outgoing.reshape(owners, SLOTS * GROUP, HD), "prefix", split_axis=0, concat_axis=0, tiled=True
    )
    *suffix, keys, values_t = suffix_attend(suffix_lengths, q_home, suffix_kv[:, :, 0], prefix_kv)
    packed = prefix_attend(arrived.reshape(owners * PAIR, HD), keys, values_t)
    back = lax.all_to_all(
        packed.reshape(owners, SENT // 2, 2, HD), "prefix", split_axis=0, concat_axis=0, tiled=True
    )
    attended = combine(slot, back.reshape(owners * SENT, HD), suffix, tensor)
    done = lax.all_to_all(attended, "tensor", split_axis=0, concat_axis=0, tiled=True)
    return jnp.swapaxes(done, 0, 1).reshape(rows, tensor * width)


def solution(mesh):
    in_specs = (
        P(("prefix", "tensor"), None),
        P("prefix", None, "tensor", None, None),
        P("prefix"),
        P("prefix", None, "tensor", None, None),
        P("prefix"),
        P(),
    )
    out_specs = P(("prefix", "tensor"), None)
    return jax.shard_map(
        on_device, mesh=mesh, in_specs=in_specs, out_specs=out_specs, check_vma=False
    )
```
